256 devices in a mesh: pair: 2 (over y_hi), grp: 8 (over z), seq: 16 (over y_lo, x, core).
Axes of the slice: x: 4, y: 4 (y_hi: 2, y_lo: 2; y = y_hi * 2 + y_lo), z: 8, core: 2. Of those that a mesh axis runs over, the one named last changes fastest.
Arguments:
- series: float32 [8, 32768, 64], P('grp', 'seq', 'pair'), may hold values from -8 to 8
- time_blocks: int32 [8, 16], P('grp'), may hold values from 0 to 127
- freq_blocks: int32 [8, 16], P('grp'), may hold values from 0 to 127
- positives: int32 [8], replicated, may hold values from 0 to 7, each once
- conv_weight: bfloat16 [2, 1024, 512], P('pair'), may hold values from -0.25 to 0.25
- proj_weight: bfloat16 [2, 1024, 128], P('pair'), may hold values from -0.1875 to 0.1875
Outputs:
- encoded: bfloat16 [2, 8, 16384, 1024], P('pair', 'grp', 'seq')
- loss_value: float32 [], replicated
- grad_conv: float32 [2, 1024, 512], P('pair', ('grp', 'seq'))
- grad_proj: float32 [2, 1024, 128], P('pair', 'grp')
The draws below stay inside these ranges and needn't reach their ends.
Inputs may be any that keep to these rules, and one draw needn't show every extreme that they name: `positives`: each of 0 to 7 stands once.
All inputs are finite; a program needn't handle non-finite values.
Results may differ from the reference program's by a relative error of at most 0.0042.
Values may be sent and summed in bfloat16 or wider, within the bound.
A program may use at most 128 MiB of HBM per device.

```python
import math
import jax
import jax.numpy as jnp
from jax import lax

C = 64
H = 1024
E = 128
K = 8
SEQLEN = 32768
B = 8
MBLK = 256
NBLK = 128
NMASK = 16


def draw_series(key, part):
    key_noise, key_scale, key_common, key_taps, key_mix, key_sign = jax.random.split(jax.random.fold_in(key, 7), 6)
    scales = jnp.exp(jax.random.uniform(key_scale, (B, 1, C), jnp.float32, math.log(0.3), math.log(3.0)))
    mixing = jnp.exp(jax.random.uniform(key_mix, (B, 1, C), jnp.float32, math.log(1.0), math.log(3.0)))
    flips = jax.random.uniform(key_sign, (B, 1, C), jnp.float32, 0.0, 1.0)
    mixing = jnp.where(flips < 0.5, -mixing, mixing)
    taps = jax.random.normal(key_taps, (B, 8), jnp.float32) / math.sqrt(8.0)
    source = jax.random.normal(key_common, (B, SEQLEN), jnp.float32)
    common = taps[:, 0:1] * source
    for offset in range(1, 8):
        common = common + taps[:, offset:offset + 1] * jnp.roll(source, offset, axis=1)
    progress = jnp.arange(SEQLEN, dtype=jnp.float32) / SEQLEN
    envelope = jnp.exp(math.log(3.0) * (progress - 1.0))[None, :, None]
    fluctuation = jax.random.truncated_normal(key_noise, -4.0, 4.0, (B, SEQLEN, C), jnp.float32)
    values = (fluctuation * scales + mixing * common[:, :, None]) * envelope
    return jnp.clip(values, -8.0, 8.0)


def set_ends(entries, stream_key, low, largest):
    extent = entries.shape
    spot = [jax.random.randint(jax.random.fold_in(stream_key, axis), (), 0, extent[axis]) for axis in range(len(extent))]
    entries = entries.at[tuple(spot)].set(low)
    longest = extent.index(max(extent))
    spot[longest] = (spot[longest] + 1) % extent[longest]
    return entries.at[tuple(spot)].set(largest)


def block_scale(key, dims, shards, least, high):
    def one(axis_at, blocks):
        heights = jax.random.uniform(jax.random.fold_in(jax.random.fold_in(key, 6), axis_at), (blocks,), jnp.float32, least / len(shards), high / len(shards))
        return jnp.repeat(jnp.exp(heights), dims[axis_at] // blocks).reshape((-1,) + (1,) * (len(dims) - axis_at - 1))

    factor_of = one(*shards[0])
    for cut in shards[1:]:
        factor_of = factor_of * one(*cut)
    return factor_of


def centred(stream_key, extent, scale, bound, cuts=(), held_as=jnp.bfloat16):
    array = jax.random.normal(stream_key, extent, jnp.float32) * scale
    if len(cuts) > 0:
        array = block_scale(stream_key, extent, cuts, -0.22, 0.18) * array
    return jnp.clip(array, min=-bound, max=bound).astype(held_as)


def setup_inputs(seed: int = 0) -> dict:
    streams_of = jax.random.split(jax.random.key(seed), 7)
    series = draw_series(jax.random.fold_in(streams_of[6], 71), 0)
    time_blocks = set_ends(jax.random.randint(streams_of[1], (B, NMASK), 0, NBLK), jax.random.fold_in(streams_of[1], 1), 0, NBLK - 1).astype(jnp.int32)
    freq_blocks = set_ends(jax.random.randint(streams_of[2], (B, NMASK), 0, NBLK), jax.random.fold_in(streams_of[2], 1), 0, NBLK - 1).astype(jnp.int32)
    positives = jax.random.permutation(streams_of[3], B).astype(jnp.int32)
    conv_weight = centred(streams_of[4], (2, H, K * C), (K * C) ** -0.5, 0.25, ((0, 2),))
    proj_weight = centred(streams_of[5], (2, H, E), H ** -0.5, 0.1875, ((0, 2),))
    return {"series": series, "time_blocks": time_blocks, "freq_blocks": freq_blocks, "positives": positives, "conv_weight": conv_weight, "proj_weight": proj_weight}


TAU = 0.2
LOSS_SCALE = 256.0

def gelu_slope(values):
    output, pullback = jax.vjp(lambda argument: jax.nn.gelu(argument, approximate=True), values)
    return (output, pullback(jnp.ones_like(values))[0])

def embed(pooled, projection):
    latent = jnp.dot(pooled, projection, precision=lax.Precision.HIGHEST)
    return latent * lax.rsqrt(lax.optimization_barrier(jnp.sum(latent * latent, axis=1, keepdims=True)) + 1e-06)

def contrast(time_emb, freq_emb, positives):
    logits = jnp.dot(time_emb, freq_emb.T, precision=lax.Precision.HIGHEST) / TAU
    number = logits.shape[0]
    target = (positives[:, None] == jnp.arange(number, dtype=jnp.int32)[None, :]).astype(logits.dtype)
    exponent = jnp.exp(logits)
    row_lse = jnp.log(lax.optimization_barrier(jnp.sum(exponent, axis=1)))
    col_lse = jnp.log(lax.optimization_barrier(jnp.sum(exponent, axis=0)))
    picked = jnp.sum(target * logits)
    return (jnp.sum(row_lse) + jnp.sum(col_lse) - 2.0 * picked) / (2.0 * number)

def reference(series, time_blocks, freq_blocks, positives, conv_weight, proj_weight):
    position = jnp.arange(SEQLEN, dtype=jnp.int32) // MBLK

    def keep_mask(blocks):
        listed = jnp.any(blocks[:, :, None] == position[None, None, :], axis=1)
        return jnp.where(listed, 0.0, 1.0).astype(jnp.bfloat16)[:, :, None]
    time_in = series.astype(jnp.bfloat16) * keep_mask(time_blocks)
    spectrum = jnp.fft.fft(series, axis=1)
    real_part = jnp.real(spectrum)
    imag_part = jnp.imag(spectrum)
    energy = (real_part * real_part + imag_part * imag_part) / SEQLEN
    freq_in = jnp.sqrt(1.0 + energy).astype(jnp.bfloat16) * keep_mask(freq_blocks)
    half_rim = K // 2

    def patch_rows(signal):
        padded = jnp.pad(signal, ((half_rim, half_rim), (0, 0)))
        return jnp.concatenate([padded[offset:offset + SEQLEN] for offset in range(K)], axis=1)

    def encode(inputs, weight):

        def single(signal):
            patches = patch_rows(signal)
            preact = lax.dot_general(patches, weight, (((1,), (1,)), ((), ())), preferred_element_type=jnp.float32)
            active = jax.nn.gelu(preact, approximate=True)
            pairs = active.reshape(SEQLEN // 2, 2, H)
            halved = ((pairs[:, 0] + pairs[:, 1]) * 0.5).astype(jnp.bfloat16)
            return (halved, lax.optimization_barrier(jnp.mean(active, axis=0)))
        return lax.map(single, inputs)

    def conv_grad(inputs, weight, scaled):

        def accumulate(running, element):
            signal, factor = element
            patches = patch_rows(signal)
            preact = lax.dot_general(patches, weight, (((1,), (1,)), ((), ())), preferred_element_type=jnp.float32)
            _, slopes = gelu_slope(preact)
            upstream = (factor[None, :] * slopes).astype(jnp.bfloat16)
            update = lax.dot_general(upstream, patches, (((0,), (0,)), ((), ())), preferred_element_type=jnp.float32)
            return (running + update, None)
        result, _ = lax.scan(accumulate, jnp.zeros((H, K * C), jnp.float32), (inputs, scaled))
        return result
    enc_time, pool_time = encode(time_in, conv_weight[0])
    enc_freq, pool_freq = encode(freq_in, conv_weight[1])
    proj_time = proj_weight[0].astype(jnp.float32)
    proj_freq = proj_weight[1].astype(jnp.float32)
    emb_time, pull_time = jax.vjp(embed, pool_time, proj_time)
    emb_freq, pull_freq = jax.vjp(embed, pool_freq, proj_freq)
    loss_value, emb_grads = jax.value_and_grad(contrast, argnums=(0, 1))(emb_time, emb_freq, positives)
    dpool_time, dproj_time = pull_time(emb_grads[0] * LOSS_SCALE)
    dpool_freq, dproj_freq = pull_freq(emb_grads[1] * LOSS_SCALE)
    grad_time = conv_grad(time_in, conv_weight[0], dpool_time / SEQLEN)
    grad_freq = conv_grad(freq_in, conv_weight[1], dpool_freq / SEQLEN)
    encoded = jnp.stack([enc_time, enc_freq])
    grad_conv = jnp.stack([grad_time, grad_freq])
    grad_proj = jnp.stack([dproj_time, dproj_freq])
    return (encoded, loss_value, grad_conv, grad_proj)
```

```python
import functools
import math

import jax
import jax.numpy as jnp
import numpy as np
from jax import lax
from jax.experimental import pallas as pl
from jax.experimental.pallas import tpu as pltpu
from jax.sharding import PartitionSpec as P

MESH = pl.DeviceIdType.MESH
F32 = jnp.float32
BF16 = jnp.bfloat16
HIGHEST = lax.Precision.HIGHEST

C = 64
H = 1024
E = 128
K = 8
SEQLEN = 32768
NSEQ = 16
NGRP = 8
NPAIR = 2
OWN = 2
SPAN = SEQLEN // NSEQ
PAIRS = SPAN // 2
BLOCKS = SPAN // 256
TAU = 0.2
LOSS_SCALE = 256.0
GELU_A = math.sqrt(2.0 / math.pi)
GELU_B = 0.044715 * GELU_A
CHIPS = NSEQ // 2
HB = 256


def split(values):
    high = values.astype(np.float32).astype(BF16)
    low = (values - high.astype(np.float64)).astype(np.float32).astype(BF16)
    return high, low


def transform_tables():
    row = np.arange(256)
    a = (row // 16) * 16 + 2 * (row % 8) + (row % 16) // 8
    col = np.arange(256)
    k1 = 2 * (col % 128) + col // 128
    first = 2 * np.pi * ((a[:, None] * k1[None, :]) % 256) / 256
    first = np.concatenate([np.cos(first), -np.sin(first)], axis=1)
    b = np.arange(128)
    turn = 2 * np.pi * (b[:, None] * k1[None, :]) / SEQLEN
    turn = np.concatenate([np.cos(turn), np.sin(turn)], axis=1).astype(np.float32)
    k2 = np.arange(128)
    second = 2 * np.pi * ((k2[:, None] * b[None, :]) % 128) / 128
    cos, sin = np.cos(second), np.sin(second)
    second = np.block([[cos, sin], [-sin, cos]])
    pick = np.zeros((2, 128, 256), np.float32)
    for odd_row in range(2):
        for step in range(128):
            pick[odd_row, step, 128 * (step % 2) + 64 * odd_row + step // 2] = 1.0
    return (*split(first), turn, *split(second), pick.astype(BF16))


def dot3(a, b_high, b_low, a_low=None):
    dot = functools.partial(jnp.dot, preferred_element_type=F32)
    return dot(a, b_high) + (dot(a, b_low) + dot(a_low, b_high))


def views_kernel(
    send, first_h, first_l, turn, second_h, second_l, pick,
    feat, halo,
    series, rows, time_main, time_halo, freq_main, freq_halo,
    s1, r1, s2, r2, s3, r3,
):
    me = lax.axis_index("seq")
    branch = lax.axis_index("pair")
    other = 1 - branch

    barrier = pltpu.get_barrier_semaphore()

    def greet(i, _):
        @pl.when(i > 0)
        def _():
            peer = lax.rem(me + i, NSEQ)
            pl.semaphore_signal(barrier, 1, device_id={"seq": peer}, device_id_type=MESH)

        peer = lax.rem(me + i, NSEQ)
        pl.semaphore_signal(barrier, 1, device_id={"pair": other, "seq": peer}, device_id_type=MESH)
        return 0

    lax.fori_loop(0, NSEQ, greet, 0)
    pl.semaphore_wait(barrier, 2 * NSEQ - 1)

    def series_copy(i, dst):
        return pltpu.make_async_remote_copy(
            src_ref=send.at[lax.rem(me + i, NSEQ)], dst_ref=series.at[dst],
            send_sem=s1.at[i], recv_sem=r1.at[i],
            device_id={"seq": lax.rem(me + i, NSEQ)}, device_id_type=MESH)

    def start_series(i, _):
        series_copy(i, me).start()
        return 0

    lax.fori_loop(1, NSEQ, start_series, 0)
    series[me] = send[me]

    def wait_series(i, _):
        series_copy(i, lax.rem(me - i + NSEQ, NSEQ)).wait_recv()
        return 0

    lax.fori_loop(1, NSEQ, wait_series, 0)

    lane = lax.broadcasted_iota(jnp.int32, (NSEQ, 128), 1)

    def pack(values, main, edge):
        parts = [v.reshape(NSEQ, BLOCKS, 256) for v in values]
        block = jnp.concatenate(parts, axis=1).astype(BF16)
        main[:, 0] = block[:, :, :128]
        main[:, 1] = block[:, :, 128:]
        for c in range(OWN):
            for half in range(2):
                columns = slice(128 * half, 128 * (half + 1))
                rows[...] = values[c][:, columns]
                low = rows[pl.ds(0, NSEQ, stride=BLOCKS), :]
                high = rows[pl.ds(BLOCKS - 1, NSEQ, stride=BLOCKS), :]
                before = pltpu.roll(high, 1, 0)
                after = pltpu.roll(low, NSEQ - 1, 0)
                both = jnp.where(lane >= 64, before, after)
                for d in range(NSEQ):
                    edge[d, c:c + 1, columns] = both[d:d + 1]

    def view_copies(view, i, main, edge, slot):
        peer = lax.rem(me + i, NSEQ)
        target = {"pair": view, "seq": peer}
        n = view * NSEQ + i
        return (
            pltpu.make_async_remote_copy(
                src_ref=main.at[peer], dst_ref=feat.at[slot], send_sem=s2.at[n],
                recv_sem=r2.at[branch * NSEQ + i], device_id=target, device_id_type=MESH),
            pltpu.make_async_remote_copy(
                src_ref=edge.at[peer], dst_ref=halo.at[slot], send_sem=s3.at[n],
                recv_sem=r3.at[branch * NSEQ + i], device_id=target, device_id_type=MESH),
        )

    mine = branch * NSEQ + me

    def start_view(view, main, edge):
        def step(i, _):
            @pl.when(jnp.logical_or(i > 0, branch != view))
            def _():
                for copy in view_copies(view, i, main, edge, mine):
                    copy.start()
            return 0

        lax.fori_loop(0, NSEQ, step, 0)

        @pl.when(branch == view)
        def _():
            feat[mine] = main[me]
            halo[mine] = edge[me]

    even = [series[:, c, 0:8, :].reshape(128, 128) for c in range(OWN)]
    odd = [series[:, c, 8:16, :].reshape(128, 128) for c in range(OWN)]
    views = [
        jnp.dot(even[c].astype(BF16), pick[0], preferred_element_type=F32)
        + jnp.dot(odd[c].astype(BF16), pick[1], preferred_element_type=F32)
        for c in range(OWN)
    ]
    pack(views, time_main, time_halo)
    start_view(0, time_main, time_halo)

    turned = []
    for c in range(OWN):
        whole = series[:, c].reshape(256, 128)
        flat = jnp.concatenate([whole[:128].T, whole[128:].T], axis=1)
        high = flat.astype(BF16)
        low = (flat - high.astype(F32)).astype(BF16)
        part = dot3(high, first_h[...], first_l[...], low)
        re, im = part[:, :256], part[:, 256:]
        cos, sin = turn[:, :256], turn[:, 256:]
        turned.append(jnp.concatenate([re * cos + im * sin, im * cos - re * sin], axis=0))
    powers = []
    for c in range(OWN):
        high = turned[c].astype(BF16)
        low = (turned[c] - high.astype(F32)).astype(BF16)
        dot = functools.partial(jnp.dot, preferred_element_type=F32)
        spec = dot(second_h[...], high) + (dot(second_h[...], low) + dot(second_l[...], high))
        re, im = spec[:128], spec[128:]
        powers.append(jnp.sqrt(1.0 + (re * re + im * im) * (1.0 / SEQLEN)))
    pack(powers, freq_main, freq_halo)
    start_view(1, freq_main, freq_halo)

    def wait_view(i, _):
        from_own = branch * NSEQ + lax.rem(me - i + NSEQ, NSEQ)
        from_other = other * NSEQ + lax.rem(me - i + NSEQ, NSEQ)

        def arrivals(source, slot):
            peer = lax.rem(me - i + NSEQ, NSEQ)
            target = {"pair": source, "seq": peer}
            return (
                pltpu.make_async_remote_copy(
                    src_ref=freq_main.at[peer], dst_ref=feat.at[slot], send_sem=s2.at[i],
                    recv_sem=r2.at[source * NSEQ + i], device_id=target, device_id_type=MESH),
                pltpu.make_async_remote_copy(
                    src_ref=freq_halo.at[peer], dst_ref=halo.at[slot], send_sem=s3.at[i],
                    recv_sem=r3.at[source * NSEQ + i], device_id=target, device_id_type=MESH),
            )

        @pl.when(i > 0)
        def _():
            for copy in arrivals(branch, from_own):
                copy.wait_recv()

        for copy in arrivals(other, from_other):
            copy.wait_recv()
        return 0

    lax.fori_loop(0, NSEQ, wait_view, 0)

    def wait_sends(i, _):
        @pl.when(i > 0)
        def _():
            series_copy(i, me).wait_send()

        for view, main, edge in ((0, time_main, time_halo), (1, freq_main, freq_halo)):
            @pl.when(jnp.logical_or(i > 0, branch != view))
            def _():
                for copy in view_copies(view, i, main, edge, mine):
                    copy.wait_send()
        return 0

    lax.fori_loop(0, NSEQ, wait_sends, 0)


def make_views(series):
    send = series[0].T.reshape(NSEQ, OWN, BLOCKS, 2, 128).transpose(0, 1, 3, 2, 4)
    send = send.reshape(NSEQ, OWN, 16, 128)
    vmem = pl.BlockSpec(memory_space=pltpu.VMEM)
    tables = [jnp.asarray(t) for t in transform_tables()]
    sources = NPAIR * NSEQ
    return pl.pallas_call(
        views_kernel,
        out_shape=(
            jax.ShapeDtypeStruct((sources, 2, 16, 128), BF16),
            jax.ShapeDtypeStruct((sources, OWN, 256), F32),
        ),
        in_specs=[vmem] * 7,
        out_specs=(vmem, vmem),
        scratch_shapes=[
            pltpu.VMEM((NSEQ, OWN, 16, 128), F32),
            pltpu.VMEM((128, 128), F32),
            pltpu.VMEM((NSEQ, 2, 16, 128), BF16),
            pltpu.VMEM((NSEQ, OWN, 256), F32),
            pltpu.VMEM((NSEQ, 2, 16, 128), BF16),
            pltpu.VMEM((NSEQ, OWN, 256), F32),
            pltpu.SemaphoreType.DMA((NSEQ,)),
            pltpu.SemaphoreType.DMA((NSEQ,)),
            pltpu.SemaphoreType.DMA((sources,)),
            pltpu.SemaphoreType.DMA((sources,)),
            pltpu.SemaphoreType.DMA((sources,)),
            pltpu.SemaphoreType.DMA((sources,)),
        ],
        compiler_params=pltpu.CompilerParams(collective_id=0, has_side_effects=True),
        name="views",
    )(send, *tables)


ROWS = 128


def encoder_kernel(
    time_blocks, freq_blocks, feat, halo, weight,
    encoded, sums, grads,
    tall, edges, wide, turned, across, patches, patches_t, slopes, total,
):
    @pl.when(pl.program_id(0) == 0)
    def _():
        me = lax.axis_index("seq")
        is_time = lax.axis_index("pair") == 0
        listed = [jnp.where(is_time, time_blocks[0, n], freq_blocks[0, n]) for n in range(16)]

        def keep(q):
            block = me * BLOCKS + q
            hit = listed[0] == block
            for n in range(1, 16):
                hit = jnp.logical_or(hit, listed[n] == block)
            drop = jnp.logical_or(hit, jnp.logical_or(block < 0, block >= NSEQ * BLOCKS))
            return jnp.where(drop, 0.0, 1.0).astype(F32)

        for parity in range(2):
            tall[parity * 512:(parity + 1) * 512, :] = (
                feat[:, parity].astype(F32).reshape(512, 128))
            for source in range(NPAIR * NSEQ):
                edges[parity * C + OWN * source:parity * C + OWN * (source + 1), :] = (
                    halo[source, :, parity * 128:(parity + 1) * 128])
        side = lax.broadcasted_iota(jnp.int32, (128, 128), 1)
        rim = edges[...].astype(BF16).astype(F32) * jnp.where(side >= 64, keep(-1), keep(BLOCKS))
        wide[:, 0:128] = rim
        wide[:, 128 + PAIRS:256 + PAIRS] = rim
        rim_t = rim.T
        turned[0:8, :] = rim_t[120:128]
        turned[8 + PAIRS:16 + PAIRS, :] = rim_t[0:8]
        for q in range(BLOCKS):
            piece = tall[pl.ds(q, 128, stride=BLOCKS), :] * keep(q)
            wide[:, 128 * (q + 1):128 * (q + 2)] = piece
            turned[8 + 128 * q:8 + 128 * (q + 1), :] = piece.T
        across[...] = pltpu.roll(turned[...], 64, 1)
        low = lax.broadcasted_iota(jnp.int32, (ROWS, 128), 1) < 64
        for j in range(K // 2):
            columns = slice(128 * j, 128 * (j + 1))
            for r in range(PAIRS // ROWS):
                at = 8 + j - 2 + ROWS * r
                patches[r, 0:ROWS, columns] = turned[at:at + ROWS, :].astype(BF16)
                patches[r, ROWS:2 * ROWS, columns] = jnp.where(
                    low, across[at:at + ROWS, :], across[at + 1:at + 1 + ROWS, :]).astype(BF16)
        shifted = []
        for d in range(-2, 3):
            whole = wide[...]
            if d != 0:
                whole = pltpu.roll(whole, (-d) % (256 + PAIRS), 1)
            part = whole[:, 128:128 + PAIRS].astype(BF16)
            j = d + 2
            if j < K // 2:
                patches_t[128 * j:128 * (j + 1), 0:PAIRS] = part
                patches_t[128 * j:128 * j + 64, PAIRS:] = part[64:]
            if j > 0:
                patches_t[128 * (j - 1) + 64:128 * j, PAIRS:] = part[:64]

    total[...] = jnp.zeros_like(total)
    weights = weight[0]

    def piece(r, _):
        preact = lax.dot_general(
            patches[r], weights, (((1,), (1,)), ((), ())), preferred_element_type=F32)
        square = preact * preact
        inner = preact * (GELU_A + GELU_B * square)
        gate = 0.5 + 0.5 * jnp.tanh(inner)
        active = preact * gate
        slope = gate + active * ((1.0 - gate) * (2.0 * GELU_A + (6.0 * GELU_B) * square))
        pair = active[:ROWS] + active[ROWS:]
        encoded[0, 0, pl.ds(r * ROWS, ROWS), :] = (pair * 0.5).astype(BF16)
        total[...] += jnp.sum(pair.reshape(ROWS // 8, 8, HB), axis=0)
        slope = slope.astype(BF16)
        slopes[pl.ds(r * ROWS, ROWS), :] = slope[:ROWS]
        slopes[pl.ds(PAIRS + r * ROWS, ROWS), :] = slope[ROWS:]
        return 0

    lax.fori_loop(0, PAIRS // ROWS, piece, 0)
    sums[...] = total[...]
    grad_t = jnp.dot(patches_t[...], slopes[...], preferred_element_type=F32)
    grad = grad_t.T.reshape(2, NSEQ, 8, K * C)
    grads[...] = jnp.concatenate([grad[0], grad[1]], axis=1).reshape(
        CHIPS, 2, 16, K * C)


def encode(time_blocks, freq_blocks, feat, halo, conv_weight):
    smem = pl.BlockSpec(memory_space=pltpu.SMEM)
    sources = NPAIR * NSEQ
    return pl.pallas_call(
        encoder_kernel,
        grid=(H // HB,),
        out_shape=(
            jax.ShapeDtypeStruct((1, 1, PAIRS, H), BF16),
            jax.ShapeDtypeStruct((8, H), F32),
            jax.ShapeDtypeStruct((CHIPS, 2, 8 * NGRP, K * C), F32),
        ),
        in_specs=[
            smem,
            smem,
            pl.BlockSpec((sources, 2, 16, 128), lambda n: (0, 0, 0, 0)),
            pl.BlockSpec((sources, OWN, 256), lambda n: (0, 0, 0)),
            pl.BlockSpec((1, HB, K * C), lambda n: (0, n, 0)),
        ],
        out_specs=(
            pl.BlockSpec((1, 1, PAIRS, HB), lambda n: (0, 0, 0, n)),
            pl.BlockSpec((8, HB), lambda n: (0, n)),
            pl.BlockSpec((CHIPS, 2, 16, K * C), lambda n: (0, 0, n, 0)),
        ),
        scratch_shapes=[
            pltpu.VMEM((8 * 2 * C, 128), F32),
            pltpu.VMEM((2 * C, 128), F32),
            pltpu.VMEM((2 * C, 256 + PAIRS), F32),
            pltpu.VMEM((16 + PAIRS, 128), F32),
            pltpu.VMEM((16 + PAIRS, 128), F32),
            pltpu.VMEM((PAIRS // ROWS, 2 * ROWS, K * C), BF16),
            pltpu.VMEM((K * C, SPAN), BF16),
            pltpu.VMEM((SPAN, HB), BF16),
            pltpu.VMEM((8, HB), F32),
        ],
        compiler_params=pltpu.CompilerParams(vmem_limit_bytes=48 * 1024 * 1024),
        name="encoder",
    )(time_blocks, freq_blocks, feat, halo, conv_weight)


def reduce_kernel(
    positives, sums, grads, proj,
    conv_out, proj_out, loss_out,
    own_sum, all_sums, notes, own_notes, other_notes, own_rows, other_rows, table,
    core_in, passed, chip_in, ready, grp_in,
    s_sum, r_sum, s_own, r_own, s_oth, r_oth, s_core, r_core, s_chip, r_chip, s_grp, r_grp,
):
    me = lax.axis_index("seq")
    branch = lax.axis_index("pair")
    grp = lax.axis_index("grp")
    other = 1 - branch
    chip, core = me // 2, lax.rem(me, 2)
    sibling = me + 1 - 2 * core

    barrier = pltpu.get_barrier_semaphore()

    def greet_seq(i, _):
        pl.semaphore_signal(
            barrier, 1, device_id={"seq": lax.rem(me + i, NSEQ)}, device_id_type=MESH)
        return 0

    def greet_grp(i, _):
        peer = lax.rem(grp + i, NGRP)

        @pl.when(i > 0)
        def _():
            pl.semaphore_signal(barrier, 1, device_id={"grp": peer}, device_id_type=MESH)

        pl.semaphore_signal(
            barrier, 1, device_id={"pair": other, "grp": peer}, device_id_type=MESH)
        return 0

    lax.fori_loop(1, NSEQ, greet_seq, 0)
    lax.fori_loop(0, NGRP, greet_grp, 0)
    own_sum[...] = jnp.sum(sums[...], axis=0, keepdims=True)
    pl.semaphore_wait(barrier, NSEQ - 1 + 2 * NGRP - 1)

    def sum_copy(i, slot):
        return pltpu.make_async_remote_copy(
            src_ref=own_sum, dst_ref=all_sums.at[slot], send_sem=s_sum.at[i],
            recv_sem=r_sum.at[i], device_id={"seq": lax.rem(me + i, NSEQ)}, device_id_type=MESH)

    def start_sum(i, _):
        sum_copy(i, me).start()
        return 0

    lax.fori_loop(1, NSEQ, start_sum, 0)
    all_sums[me] = own_sum[...]

    def core_copy(i):
        j = lax.rem(chip + i, CHIPS)
        return pltpu.make_async_remote_copy(
            src_ref=grads.at[j, 1 - core], dst_ref=core_in.at[j], send_sem=s_core.at[i],
            recv_sem=r_core.at[i], device_id={"seq": sibling}, device_id_type=MESH)

    def chip_copy(i, slot):
        j = lax.rem(chip + i, CHIPS)
        return pltpu.make_async_remote_copy(
            src_ref=passed.at[j], dst_ref=chip_in.at[slot], send_sem=s_chip.at[i],
            recv_sem=r_chip.at[i], device_id={"seq": 2 * j + core}, device_id_type=MESH)

    def start_core(i, _):
        core_copy(lax.rem(i, CHIPS)).start()
        return 0

    lax.fori_loop(1, CHIPS + 1, start_core, 0)
    table[...] = proj[0].astype(F32)

    def pass_on(i, _):
        core_copy(i).wait_recv()
        j = lax.rem(chip + i, CHIPS)
        passed[j] = grads[j, core] + core_in[j]
        chip_copy(i, chip).start()
        return 0

    lax.fori_loop(1, CHIPS, pass_on, 0)

    def wait_sum(i, _):
        sum_copy(i, lax.rem(me - i + NSEQ, NSEQ)).wait_recv()
        return 0

    lax.fori_loop(1, NSEQ, wait_sum, 0)
    pooled = jnp.sum(all_sums[...], axis=0) * (1.0 / SEQLEN)
    latent = jnp.dot(
        jnp.broadcast_to(pooled, (8, H)), table[...], precision=HIGHEST,
        preferred_element_type=F32)[0:1]
    for g in range(NGRP):
        notes[g] = jnp.concatenate([latent, pooled[:, 128 * g:128 * (g + 1)]], axis=1)

    def own_copy(i, slot):
        peer = lax.rem(grp + i, NGRP)
        return pltpu.make_async_remote_copy(
            src_ref=notes.at[peer], dst_ref=own_notes.at[slot], send_sem=s_own.at[i],
            recv_sem=r_own.at[i], device_id={"grp": peer}, device_id_type=MESH)

    def other_copy(i, slot):
        peer = lax.rem(grp + i, NGRP)
        return pltpu.make_async_remote_copy(
            src_ref=notes.at[peer], dst_ref=other_notes.at[slot], send_sem=s_oth.at[i],
            recv_sem=r_oth.at[i], device_id={"pair": other, "grp": peer}, device_id_type=MESH)

    def start_notes(i, _):
        @pl.when(i > 0)
        def _():
            own_copy(i, grp).start()

        other_copy(i, grp).start()
        return 0

    lax.fori_loop(0, NGRP, start_notes, 0)
    own_notes[grp] = notes[grp]

    def wait_notes(i, _):
        source = lax.rem(grp - i + NGRP, NGRP)

        @pl.when(i > 0)
        def _():
            own_copy(i, source).wait_recv()

        other_copy(i, source).wait_recv()
        return 0

    lax.fori_loop(0, NGRP, wait_notes, 0)
    for g in range(NGRP):
        own_rows[g:g + 1, :] = own_notes[g]
        other_rows[g:g + 1, :] = other_notes[g]
    z_own, z_other = own_rows[:, :E], other_rows[:, :E]
    r_own_ = lax.rsqrt(jnp.sum(z_own * z_own, axis=1, keepdims=True) + 1e-06)
    r_other_ = lax.rsqrt(jnp.sum(z_other * z_other, axis=1, keepdims=True) + 1e-06)
    e_own, e_other = z_own * r_own_, z_other * r_other_
    is_time = branch == 0
    time_emb = jnp.where(is_time, e_own, e_other)
    freq_emb = jnp.where(is_time, e_other, e_own)
    dot = functools.partial(
        lax.dot_general, precision=HIGHEST, preferred_element_type=F32)
    logits = dot(time_emb, freq_emb, (((1,), (1,)), ((), ()))) * (1.0 / TAU)
    row = lax.broadcasted_iota(jnp.int32, (NGRP, NGRP), 0)
    col = lax.broadcasted_iota(jnp.int32, (NGRP, NGRP), 1)
    target = jnp.zeros((NGRP, NGRP), F32)
    for i in range(NGRP):
        target = jnp.where(jnp.logical_and(row == i, col == positives[i]), 1.0, target)
    exponent = jnp.exp(logits)
    by_row = jnp.sum(exponent, axis=1, keepdims=True)
    by_col = jnp.sum(exponent, axis=0, keepdims=True)
    picked = jnp.sum(jnp.sum(target * logits, axis=1, keepdims=True), axis=0, keepdims=True)
    lse = jnp.sum(jnp.log(by_row), axis=0, keepdims=True) + jnp.sum(
        jnp.log(by_col), axis=1, keepdims=True)
    loss_out[...] = (lse - 2.0 * picked) * (1.0 / (2 * NGRP))
    slope = (exponent / by_row + exponent / by_col - 2.0 * target) * (
        LOSS_SCALE / (TAU * 2 * NGRP))
    d_time = dot(slope, freq_emb, (((1,), (0,)), ((), ())))
    d_freq = dot(slope, time_emb, (((0,), (0,)), ((), ())))
    d_emb = jnp.where(is_time, d_time, d_freq)
    inner = jnp.sum(z_own * d_emb, axis=1, keepdims=True)
    d_latent = r_own_ * d_emb - z_own * (r_own_ * r_own_ * r_own_ * inner)
    proj_out[0] = dot(own_rows[:, E:], d_latent, (((0,), (0,)), ((), ())))
    sample = lax.broadcasted_iota(jnp.int32, (NGRP, E), 0)
    d_mine = jnp.sum(jnp.where(sample == grp, d_latent, 0.0), axis=0, keepdims=True)

    core_copy(0).wait_recv()
    whole = grads[chip, core] + core_in[chip]

    def wait_chip(i, _):
        chip_copy(i, lax.rem(chip - i + CHIPS, CHIPS)).wait_recv()
        return 0

    lax.fori_loop(1, CHIPS, wait_chip, 0)
    chip_in[chip] = jnp.zeros((8 * NGRP, K * C), F32)
    for j in range(CHIPS):
        whole = whole + chip_in[j]
    for g in range(NGRP):
        at = pl.multiple_of(128 * g + 8 * me, 8)
        factor = jnp.sum(table[pl.ds(at, 8), :] * d_mine, axis=1, keepdims=True)
        ready[g] = whole[8 * g:8 * (g + 1)] * (factor * (1.0 / SEQLEN))

    def grp_copy(i, slot):
        peer = lax.rem(grp + i, NGRP)
        return pltpu.make_async_remote_copy(
            src_ref=ready.at[peer], dst_ref=grp_in.at[slot], send_sem=s_grp.at[i],
            recv_sem=r_grp.at[i], device_id={"grp": peer}, device_id_type=MESH)

    def start_grp(i, _):
        grp_copy(i, grp).start()
        return 0

    lax.fori_loop(1, NGRP, start_grp, 0)
    grp_in[grp] = ready[grp]

    def wait_grp(i, _):
        grp_copy(i, lax.rem(grp - i + NGRP, NGRP)).wait_recv()
        return 0

    lax.fori_loop(1, NGRP, wait_grp, 0)
    result = grp_in[0]
    for g in range(1, NGRP):
        result = result + grp_in[g]
    conv_out[0] = result

    def sent_seq(i, _):
        sum_copy(i, me).wait_send()
        return 0

    def sent_chip(i, _):
        core_copy(i).wait_send()

        @pl.when(i > 0)
        def _():
            chip_copy(i, chip).wait_send()
            own_copy(i, grp).wait_send()
            grp_copy(i, grp).wait_send()

        other_copy(i, grp).wait_send()
        return 0

    lax.fori_loop(1, NSEQ, sent_seq, 0)
    lax.fori_loop(0, CHIPS, sent_chip, 0)


def reduce_all(positives, sums, grads, proj_weight):
    vmem = pl.BlockSpec(memory_space=pltpu.VMEM)
    smem = pl.BlockSpec(memory_space=pltpu.SMEM)
    part = (8 * NGRP, K * C)
    dma = pltpu.SemaphoreType.DMA
    return pl.pallas_call(
        reduce_kernel,
        out_shape=(
            jax.ShapeDtypeStruct((1, 8, K * C), F32),
            jax.ShapeDtypeStruct((1, H // NGRP, E), F32),
            jax.ShapeDtypeStruct((1, 1), F32),
        ),
        in_specs=[smem, vmem, vmem, vmem],
        out_specs=(vmem, vmem, vmem),
        scratch_shapes=[
            pltpu.VMEM((1, H), F32),
            pltpu.VMEM((NSEQ, 1, H), F32),
            pltpu.VMEM((NGRP, 1, 2 * E), F32),
            pltpu.VMEM((NGRP, 1, 2 * E), F32),
            pltpu.VMEM((NGRP, 1, 2 * E), F32),
            pltpu.VMEM((NGRP, 2 * E), F32),
            pltpu.VMEM((NGRP, 2 * E), F32),
            pltpu.VMEM((H, E), F32),
            pltpu.VMEM((CHIPS, *part), F32),
            pltpu.VMEM((CHIPS, *part), F32),
            pltpu.VMEM((CHIPS, *part), F32),
            pltpu.VMEM((NGRP, 8, K * C), F32),
            pltpu.VMEM((NGRP, 8, K * C), F32),
            dma((NSEQ,)), dma((NSEQ,)),
            dma((NGRP,)), dma((NGRP,)),
            dma((NGRP,)), dma((NGRP,)),
            dma((CHIPS,)), dma((CHIPS,)),
            dma((CHIPS,)), dma((CHIPS,)),
            dma((NGRP,)), dma((NGRP,)),
        ],
        compiler_params=pltpu.CompilerParams(collective_id=1, has_side_effects=True),
        name="reduce",
    )(positives, sums, grads, proj_weight)


def body(series, time_blocks, freq_blocks, positives, conv_weight, proj_weight):
    feat, halo = make_views(series)
    encoded, sums, grads = encode(time_blocks, freq_blocks, feat, halo, conv_weight)
    conv_share, proj_share, loss = reduce_all(positives, sums, grads, proj_weight)
    return (encoded, loss[0, 0], conv_share, proj_share)


def solution(mesh):
    in_specs = (
        P("grp", "seq", "pair"),
        P("grp", None),
        P("grp", None),
        P(),
        P("pair", None, None),
        P("pair", None, None),
    )
    out_specs = (
        P("pair", "grp", "seq", None),
        P(),
        P("pair", ("grp", "seq"), None),
        P("pair", "grp", None),
    )
    return jax.shard_map(body, mesh=mesh, in_specs=in_specs, out_specs=out_specs, check_vma=False)
```

```python
import functools
import math

import jax
import jax.numpy as jnp
import numpy as np
from jax import lax
from jax.experimental import pallas as pl
from jax.experimental.pallas import tpu as pltpu
from jax.sharding import PartitionSpec as P

MESH = pl.DeviceIdType.MESH
F32 = jnp.float32
BF16 = jnp.bfloat16
HIGHEST = lax.Precision.HIGHEST

C = 64
H = 1024
E = 128
K = 8
SEQLEN = 32768
NSEQ = 16
NGRP = 8
NPAIR = 2
OWN = 2
SPAN = SEQLEN // NSEQ
PAIRS = SPAN // 2
BLOCKS = SPAN // 256
TAU = 0.2
LOSS_SCALE = 256.0
GELU_A = math.sqrt(2.0 / math.pi)
GELU_B = 0.044715 * GELU_A
CHIPS = NSEQ // 2
HB = 256
BANDS = H // HB
ROWS = 128
PIECES = PAIRS // ROWS
DEPTH = 2


def split(values):
    high = values.astype(np.float32).astype(BF16)
    low = (values - high.astype(np.float64)).astype(np.float32).astype(BF16)
    return high, low


def transform_tables():
    row = np.arange(256)
    a = (row // 16) * 16 + 2 * (row % 8) + (row % 16) // 8
    col = np.arange(256)
    k1 = 2 * (col % 128) + col // 128
    first = 2 * np.pi * ((a[:, None] * k1[None, :]) % 256) / 256
    first = np.concatenate([np.cos(first), -np.sin(first)], axis=1)
    b = np.arange(128)
    turn = 2 * np.pi * (b[:, None] * k1[None, :]) / SEQLEN
    turn = np.concatenate([np.cos(turn), np.sin(turn)], axis=1).astype(np.float32)
    k2 = np.arange(128)
    second = 2 * np.pi * ((k2[:, None] * b[None, :]) % 128) / 128
    cos, sin = np.cos(second), np.sin(second)
    second = np.block([[cos, sin], [-sin, cos]])
    pick = np.zeros((2, 128, 256), np.float32)
    for odd_row in range(2):
        for step in range(128):
            pick[odd_row, step, 128 * (step % 2) + 64 * odd_row + step // 2] = 1.0
    return (*split(first), turn, *split(second), pick.astype(BF16))


def dot3(a, b_high, b_low, a_low=None):
    dot = functools.partial(jnp.dot, preferred_element_type=F32)
    return dot(a, b_high) + (dot(a, b_low) + dot(a_low, b_high))


def step_kernel(
    positives, time_blocks, freq_blocks, series_in, weight_in, proj_in,
    first_h_in, first_l_in, turn_in, second_h_in, second_l_in, pick_in,
    encoded, conv_out, proj_out, loss_out,
    raw, weight, proj, first_h, first_l, turn, second_h, second_l, pick,
    send, series, rows, time_main, time_halo, freq_main, freq_halo, feat, halo,
    tall, edges, wide, turned, across, patches, patches_t, held, total, grad_t,
    own_sum, all_sums, notes, own_notes, other_notes, own_rows, other_rows, table,
    grads, core_in, passed, chip_in, ready, grp_in,
    s_in, s_enc, s1, r1, s2, r2, s3, r3,
    s_sum, r_sum, s_own, r_own, s_oth, r_oth, s_core, r_core, s_chip, r_chip, s_grp, r_grp,
):
    me = lax.axis_index("seq")
    branch = lax.axis_index("pair")
    grp = lax.axis_index("grp")
    other = 1 - branch
    chip, core = me // 2, lax.rem(me, 2)
    sibling = me + 1 - 2 * core
    is_time = branch == 0

    loads = [
        pltpu.make_async_copy(src, dst, s_in.at[n])
        for n, (src, dst) in enumerate((
            (series_in, raw), (pick_in, pick), (first_h_in, first_h), (first_l_in, first_l),
            (turn_in, turn), (second_h_in, second_h), (second_l_in, second_l),
            (weight_in, weight), (proj_in, proj)))
    ]
    for load in loads:
        load.start()

    barrier = pltpu.get_barrier_semaphore()

    def greet_seq(i, _):
        peer = lax.rem(me + i, NSEQ)

        @pl.when(i > 0)
        def _():
            pl.semaphore_signal(barrier, 1, device_id={"seq": peer}, device_id_type=MESH)

        pl.semaphore_signal(barrier, 1, device_id={"pair": other, "seq": peer}, device_id_type=MESH)
        return 0

    def greet_grp(i, _):
        peer = lax.rem(grp + i, NGRP)
        pl.semaphore_signal(barrier, 1, device_id={"grp": peer}, device_id_type=MESH)
        pl.semaphore_signal(barrier, 1, device_id={"pair": other, "grp": peer}, device_id_type=MESH)
        return 0

    lax.fori_loop(0, NSEQ, greet_seq, 0)
    lax.fori_loop(1, NGRP, greet_grp, 0)

    loads[0].wait()
    for q in range(BLOCKS):
        for odd in range(2):
            at = 128 * (2 * q + odd)
            send[pl.ds(8 * odd + q, NSEQ * OWN, stride=16), :] = raw[:, at:at + 128]
    pl.semaphore_wait(barrier, 2 * NSEQ - 1 + 2 * (NGRP - 1))

    def series_copy(i, dst):
        peer = lax.rem(me + i, NSEQ)
        return pltpu.make_async_remote_copy(
            src_ref=send.at[pl.ds(pl.multiple_of(32 * peer, 32), 32)], dst_ref=series.at[dst],
            send_sem=s1.at[i], recv_sem=r1.at[i], device_id={"seq": peer}, device_id_type=MESH)

    def start_series(i, _):
        series_copy(i, me).start()
        return 0

    lax.fori_loop(1, NSEQ, start_series, 0)
    series[me] = send[pl.ds(pl.multiple_of(32 * me, 32), 32), :]
    for load in loads[1:]:
        load.wait()
    table[...] = proj[0].astype(F32)

    def wait_series(i, _):
        series_copy(i, lax.rem(me - i + NSEQ, NSEQ)).wait_recv()
        return 0

    lax.fori_loop(1, NSEQ, wait_series, 0)

    lane = lax.broadcasted_iota(jnp.int32, (NSEQ, 128), 1)

    def pack(values, main, edge):
        parts = [v.reshape(NSEQ, BLOCKS, 256) for v in values]
        block = jnp.concatenate(parts, axis=1).astype(BF16)
        main[:, 0] = block[:, :, :128]
        main[:, 1] = block[:, :, 128:]
        for c in range(OWN):
            for half in range(2):
                columns = slice(128 * half, 128 * (half + 1))
                rows[...] = values[c][:, columns]
                low = rows[pl.ds(0, NSEQ, stride=BLOCKS), :]
                high = rows[pl.ds(BLOCKS - 1, NSEQ, stride=BLOCKS), :]
                before = pltpu.roll(high, 1, 0)
                after = pltpu.roll(low, NSEQ - 1, 0)
                both = jnp.where(lane >= 64, before, after)
                for d in range(NSEQ):
                    edge[d, c:c + 1, columns] = both[d:d + 1]

    def view_copies(view, i, main, edge, slot):
        peer = lax.rem(me + i, NSEQ)
        target = {"pair": view, "seq": peer}
        n = view * NSEQ + i
        return (
            pltpu.make_async_remote_copy(
                src_ref=main.at[peer], dst_ref=feat.at[slot], send_sem=s2.at[n],
                recv_sem=r2.at[branch * NSEQ + i], device_id=target, device_id_type=MESH),
            pltpu.make_async_remote_copy(
                src_ref=edge.at[peer], dst_ref=halo.at[slot], send_sem=s3.at[n],
                recv_sem=r3.at[branch * NSEQ + i], device_id=target, device_id_type=MESH),
        )

    mine = branch * NSEQ + me

    def start_view(view, main, edge):
        def step(i, _):
            @pl.when(jnp.logical_or(i > 0, branch != view))
            def _():
                for copy in view_copies(view, i, main, edge, mine):
                    copy.start()
            return 0

        lax.fori_loop(0, NSEQ, step, 0)

        @pl.when(branch == view)
        def _():
            feat[mine] = main[me]
            halo[mine] = edge[me]

    even = [series[:, 16 * c:16 * c + 8, :].reshape(128, 128) for c in range(OWN)]
    odd = [series[:, 16 * c + 8:16 * c + 16, :].reshape(128, 128) for c in range(OWN)]
    views = [
        jnp.dot(even[c].astype(BF16), pick[0], preferred_element_type=F32)
        + jnp.dot(odd[c].astype(BF16), pick[1], preferred_element_type=F32)
        for c in range(OWN)
    ]
    pack(views, time_main, time_halo)
    start_view(0, time_main, time_halo)

    spun = []
    for c in range(OWN):
        whole = series[:, 16 * c:16 * c + 16, :].reshape(256, 128)
        flat = jnp.concatenate([whole[:128].T, whole[128:].T], axis=1)
        high = flat.astype(BF16)
        low = (flat - high.astype(F32)).astype(BF16)
        part = dot3(high, first_h[...], first_l[...], low)
        re, im = part[:, :256], part[:, 256:]
        cos, sin = turn[:, :256], turn[:, 256:]
        spun.append(jnp.concatenate([re * cos + im * sin, im * cos - re * sin], axis=0))
    powers = []
    for c in range(OWN):
        high = spun[c].astype(BF16)
        low = (spun[c] - high.astype(F32)).astype(BF16)
        dot = functools.partial(jnp.dot, preferred_element_type=F32)
        spec = dot(second_h[...], high) + (dot(second_h[...], low) + dot(second_l[...], high))
        re, im = spec[:128], spec[128:]
        powers.append(jnp.sqrt(1.0 + (re * re + im * im) * (1.0 / SEQLEN)))
    pack(powers, freq_main, freq_halo)
    start_view(1, freq_main, freq_halo)

    def wait_view(i, _):
        peer = lax.rem(me - i + NSEQ, NSEQ)

        def arrivals(source):
            slot = source * NSEQ + peer
            target = {"pair": source, "seq": peer}
            return (
                pltpu.make_async_remote_copy(
                    src_ref=freq_main.at[peer], dst_ref=feat.at[slot], send_sem=s2.at[i],
                    recv_sem=r2.at[source * NSEQ + i], device_id=target, device_id_type=MESH),
                pltpu.make_async_remote_copy(
                    src_ref=freq_halo.at[peer], dst_ref=halo.at[slot], send_sem=s3.at[i],
                    recv_sem=r3.at[source * NSEQ + i], device_id=target, device_id_type=MESH),
            )

        @pl.when(i > 0)
        def _():
            for copy in arrivals(branch):
                copy.wait_recv()

        for copy in arrivals(other):
            copy.wait_recv()
        return 0

    lax.fori_loop(0, NSEQ, wait_view, 0)

    listed = [jnp.where(is_time, time_blocks[0, n], freq_blocks[0, n]) for n in range(16)]

    def keep(q):
        block = me * BLOCKS + q
        hit = listed[0] == block
        for n in range(1, 16):
            hit = jnp.logical_or(hit, listed[n] == block)
        drop = jnp.logical_or(hit, jnp.logical_or(block < 0, block >= NSEQ * BLOCKS))
        return jnp.where(drop, 0.0, 1.0).astype(F32)

    for parity in range(2):
        tall[parity * 512:(parity + 1) * 512, :] = feat[:, parity].astype(F32).reshape(512, 128)
        for source in range(NPAIR * NSEQ):
            edges[parity * C + OWN * source:parity * C + OWN * (source + 1), :] = (
                halo[source, :, parity * 128:(parity + 1) * 128])
    side = lax.broadcasted_iota(jnp.int32, (128, 128), 1)
    rim = edges[...].astype(BF16).astype(F32) * jnp.where(side >= 64, keep(-1), keep(BLOCKS))
    wide[:, 0:128] = rim
    wide[:, 128 + PAIRS:256 + PAIRS] = rim
    rim_t = rim.T
    turned[0:8, :] = rim_t[120:128]
    turned[8 + PAIRS:16 + PAIRS, :] = rim_t[0:8]
    for q in range(BLOCKS):
        piece = tall[pl.ds(q, 128, stride=BLOCKS), :] * keep(q)
        wide[:, 128 * (q + 1):128 * (q + 2)] = piece
        turned[8 + 128 * q:8 + 128 * (q + 1), :] = piece.T
    across[...] = pltpu.roll(turned[...], 64, 1)
    low_half = lax.broadcasted_iota(jnp.int32, (ROWS, 128), 1) < 64
    for j in range(K // 2):
        columns = slice(128 * j, 128 * (j + 1))
        for r in range(PIECES):
            at = 8 + j - 2 + ROWS * r
            patches[r, 0:ROWS, columns] = turned[at:at + ROWS, :].astype(BF16)
            patches[r, ROWS:2 * ROWS, columns] = jnp.where(
                low_half, across[at:at + ROWS, :], across[at + 1:at + 1 + ROWS, :]).astype(BF16)
    for d in range(-2, 3):
        whole = wide[...]
        if d != 0:
            whole = pltpu.roll(whole, (-d) % (256 + PAIRS), 1)
        part = whole[:, 128:128 + PAIRS].astype(BF16)
        j = d + 2
        for r in range(PIECES):
            chunk = part[:, ROWS * r:ROWS * (r + 1)]
            at = 2 * ROWS * r
            if j < K // 2:
                patches_t[128 * j:128 * (j + 1), at:at + ROWS] = chunk
                patches_t[128 * j:128 * j + 64, at + ROWS:at + 2 * ROWS] = chunk[64:]
            if j > 0:
                patches_t[128 * (j - 1) + 64:128 * j, at + ROWS:at + 2 * ROWS] = chunk[:64]

    def encoded_copy(n):
        slot = lax.rem(n, 2)
        return pltpu.make_async_copy(
            held.at[slot],
            encoded.at[0, 0, :, pl.ds(pl.multiple_of(n * HB, HB), HB)], s_enc.at[slot])

    def core_copy(n):
        return pltpu.make_async_remote_copy(
            src_ref=grads.at[n, 1 - core], dst_ref=core_in.at[n], send_sem=s_core.at[n],
            recv_sem=r_core.at[n], device_id={"seq": sibling}, device_id_type=MESH)

    def chip_copy(n, i, slot):
        j = lax.rem(chip + i, CHIPS)
        return pltpu.make_async_remote_copy(
            src_ref=passed.at[n, j], dst_ref=chip_in.at[n, slot], send_sem=s_chip.at[n, i],
            recv_sem=r_chip.at[n, i], device_id={"seq": 2 * j + core}, device_id_type=MESH)

    def sum_copy(i, slot):
        return pltpu.make_async_remote_copy(
            src_ref=own_sum, dst_ref=all_sums.at[slot], send_sem=s_sum.at[i],
            recv_sem=r_sum.at[i], device_id={"seq": lax.rem(me + i, NSEQ)}, device_id_type=MESH)

    def pass_on(n):
        core_copy(n).wait_recv()

        def one(i, _):
            j = lax.rem(chip + i, CHIPS)
            passed[n, j] = grads[n, core, j] + core_in[n, j]
            chip_copy(n, i, chip).start()
            return 0

        lax.fori_loop(1, CHIPS, one, 0)

    def forward(n, _):
        weights = weight[0, pl.ds(pl.multiple_of(n * HB, HB), HB), :]

        @pl.when(n >= 2)
        def _():
            encoded_copy(n).wait()

        slot = lax.rem(n, 2)

        def product(r):
            return lax.dot_general(
                patches[r], weights, (((1,), (1,)), ((), ())), preferred_element_type=F32)

        count = jnp.zeros((8, HB), F32)
        kept = []
        preact = product(0)
        for r in range(PIECES):
            following = product(r + 1) if r + 1 < PIECES else None
            square = preact * preact
            inner = preact * (GELU_A + GELU_B * square)
            half = 0.5 * jnp.tanh(inner)
            gate = 0.5 + half
            active = preact * gate
            slope = gate + active * ((0.5 - half) * (2.0 * GELU_A + (6.0 * GELU_B) * square))
            pair = active[:ROWS] + active[ROWS:]
            held[slot, r * ROWS:(r + 1) * ROWS, :] = (pair * 0.5).astype(BF16)
            count = count + jnp.sum(pair.reshape(ROWS // 8, 8, HB), axis=0)
            kept.append(slope.astype(BF16))
            if len(kept) == DEPTH:
                at = 2 * ROWS * (r + 1 - DEPTH)
                update = jnp.dot(
                    patches_t[:, at:at + 2 * ROWS * DEPTH], jnp.concatenate(kept, axis=0),
                    preferred_element_type=F32)
                if r + 1 == DEPTH:
                    grad_t[...] = update
                else:
                    grad_t[...] += update
                kept = []
            preact = following
        total[n] = count
        encoded_copy(n).start()

        @pl.when(n == BANDS - 1)
        def _():
            for band in range(BANDS):
                own_sum[:, HB * band:HB * (band + 1)] = jnp.sum(
                    total[band], axis=0, keepdims=True)

            def start_sum(i, _):
                sum_copy(i, me).start()
                return 0

            lax.fori_loop(1, NSEQ, start_sum, 0)
            all_sums[me] = own_sum[...]

        grad = grad_t[...].T.reshape(2, CHIPS, 2, 8, K * C)
        for e in range(2):
            grads[n, e, :, 0:8, :] = grad[0, :, e]
            grads[n, e, :, 8:16, :] = grad[1, :, e]
        core_copy(n).start()

        @pl.when(n >= 1)
        def _():
            pass_on(n - 1)

        return 0

    lax.fori_loop(0, BANDS, forward, 0)

    def wait_sum(i, _):
        sum_copy(i, lax.rem(me - i + NSEQ, NSEQ)).wait_recv()
        return 0

    lax.fori_loop(1, NSEQ, wait_sum, 0)
    pooled = jnp.sum(all_sums[...], axis=0) * (1.0 / SEQLEN)
    latent = jnp.dot(
        jnp.broadcast_to(pooled, (8, H)), table[...], precision=HIGHEST,
        preferred_element_type=F32)[0:1]
    for g in range(NGRP):
        notes[g] = jnp.concatenate([latent, pooled[:, 128 * g:128 * (g + 1)]], axis=1)

    def own_copy(i, slot):
        peer = lax.rem(grp + i, NGRP)
        return pltpu.make_async_remote_copy(
            src_ref=notes.at[peer], dst_ref=own_notes.at[slot], send_sem=s_own.at[i],
            recv_sem=r_own.at[i], device_id={"grp": peer}, device_id_type=MESH)

    def other_copy(i, slot):
        peer = lax.rem(grp + i, NGRP)
        return pltpu.make_async_remote_copy(
            src_ref=notes.at[peer], dst_ref=other_notes.at[slot], send_sem=s_oth.at[i],
            recv_sem=r_oth.at[i], device_id={"pair": other, "grp": peer}, device_id_type=MESH)

    def start_notes(i, _):
        @pl.when(i > 0)
        def _():
            own_copy(i, grp).start()

        other_copy(i, grp).start()
        return 0

    lax.fori_loop(0, NGRP, start_notes, 0)
    own_notes[grp] = notes[grp]
    pass_on(BANDS - 1)

    def wait_notes(i, _):
        source = lax.rem(grp - i + NGRP, NGRP)

        @pl.when(i > 0)
        def _():
            own_copy(i, source).wait_recv()

        other_copy(i, source).wait_recv()
        return 0

    lax.fori_loop(0, NGRP, wait_notes, 0)
    for g in range(NGRP):
        own_rows[g:g + 1, :] = own_notes[g]
        other_rows[g:g + 1, :] = other_notes[g]
    z_own, z_other = own_rows[:, :E], other_rows[:, :E]
    scale = lax.rsqrt(jnp.sum(z_own * z_own, axis=1, keepdims=True) + 1e-06)
    scale_other = lax.rsqrt(jnp.sum(z_other * z_other, axis=1, keepdims=True) + 1e-06)
    e_own, e_other = z_own * scale, z_other * scale_other
    time_emb = jnp.where(is_time, e_own, e_other)
    freq_emb = jnp.where(is_time, e_other, e_own)
    dot = functools.partial(lax.dot_general, precision=HIGHEST, preferred_element_type=F32)
    logits = dot(time_emb, freq_emb, (((1,), (1,)), ((), ()))) * (1.0 / TAU)
    row = lax.broadcasted_iota(jnp.int32, (NGRP, NGRP), 0)
    col = lax.broadcasted_iota(jnp.int32, (NGRP, NGRP), 1)
    target = jnp.zeros((NGRP, NGRP), F32)
    for i in range(NGRP):
        target = jnp.where(jnp.logical_and(row == i, col == positives[i]), 1.0, target)
    exponent = jnp.exp(logits)
    by_row = jnp.sum(exponent, axis=1, keepdims=True)
    by_col = jnp.sum(exponent, axis=0, keepdims=True)
    slope = (exponent / by_row + exponent / by_col - 2.0 * target) * (
        LOSS_SCALE / (TAU * 2 * NGRP))
    d_time = dot(slope, freq_emb, (((1,), (0,)), ((), ())))
    d_freq = dot(slope, time_emb, (((0,), (0,)), ((), ())))
    d_emb = jnp.where(is_time, d_time, d_freq)
    along = jnp.sum(z_own * d_emb, axis=1, keepdims=True)
    d_latent = scale * d_emb - z_own * (scale * scale * scale * along)
    sample = lax.broadcasted_iota(jnp.int32, (NGRP, E), 0)
    d_mine = jnp.sum(jnp.where(sample == grp, d_latent, 0.0), axis=0, keepdims=True)

    def wait_chip(i, _):
        for n in range(BANDS):
            chip_copy(n, i, lax.rem(chip - i + CHIPS, CHIPS)).wait_recv()
        return 0

    lax.fori_loop(1, CHIPS, wait_chip, 0)
    for n in range(BANDS):
        chip_in[n, chip] = grads[n, core, chip] + core_in[n, chip]
        whole = chip_in[n, 0]
        for j in range(1, CHIPS):
            whole = whole + chip_in[n, j]
        for k in range(2):
            g = 2 * n + k
            at = pl.multiple_of(128 * g + 8 * me, 8)
            factor = jnp.sum(table[pl.ds(at, 8), :] * d_mine, axis=1, keepdims=True)
            ready[g] = whole[8 * k:8 * (k + 1)] * (factor * (1.0 / SEQLEN))

    def grp_copy(i, slot):
        peer = lax.rem(grp + i, NGRP)
        return pltpu.make_async_remote_copy(
            src_ref=ready.at[peer], dst_ref=grp_in.at[slot], send_sem=s_grp.at[i],
            recv_sem=r_grp.at[i], device_id={"grp": peer}, device_id_type=MESH)

    def start_grp(i, _):
        grp_copy(i, grp).start()
        return 0

    lax.fori_loop(1, NGRP, start_grp, 0)
    grp_in[grp] = ready[grp]

    picked = jnp.sum(jnp.sum(target * logits, axis=1, keepdims=True), axis=0, keepdims=True)
    lse = jnp.sum(jnp.log(by_row), axis=0, keepdims=True) + jnp.sum(
        jnp.log(by_col), axis=1, keepdims=True)
    loss_out[...] = (lse - 2.0 * picked) * (1.0 / (2 * NGRP))
    proj_out[0] = dot(own_rows[:, E:], d_latent, (((0,), (0,)), ((), ())))
    for n in range(BANDS - 2, BANDS):
        encoded_copy(n).wait()

    def sent_seq(i, _):
        for view, main, edge in ((0, time_main, time_halo), (1, freq_main, freq_halo)):
            @pl.when(jnp.logical_or(i > 0, branch != view))
            def _():
                for copy in view_copies(view, i, main, edge, mine):
                    copy.wait_send()

        @pl.when(i > 0)
        def _():
            series_copy(i, me).wait_send()
            sum_copy(i, me).wait_send()
        return 0

    def sent_grp(i, _):
        @pl.when(i > 0)
        def _():
            for n in range(BANDS):
                chip_copy(n, i, chip).wait_send()
            own_copy(i, grp).wait_send()
            grp_copy(i, grp).wait_send()

        other_copy(i, grp).wait_send()
        return 0

    lax.fori_loop(0, NSEQ, sent_seq, 0)
    for n in range(BANDS):
        core_copy(n).wait_send()

    def wait_grp(i, _):
        grp_copy(i, lax.rem(grp - i + NGRP, NGRP)).wait_recv()
        return 0

    lax.fori_loop(1, NGRP, wait_grp, 0)
    result = grp_in[0]
    for g in range(1, NGRP):
        result = result + grp_in[g]
    conv_out[0] = result
    lax.fori_loop(0, CHIPS, sent_grp, 0)


def body(series, time_blocks, freq_blocks, positives, conv_weight, proj_weight):
    vmem = pl.BlockSpec(memory_space=pltpu.VMEM)
    smem = pl.BlockSpec(memory_space=pltpu.SMEM)
    anywhere = pl.BlockSpec(memory_space=pltpu.HBM)
    tables = [jnp.asarray(t) for t in transform_tables()]
    sources = NPAIR * NSEQ
    dma = pltpu.SemaphoreType.DMA
    part = (BANDS, CHIPS, 16, K * C)
    main, edge = (NSEQ, 2, 16, 128), (NSEQ, OWN, 256)
    encoded, conv_share, proj_share, loss = pl.pallas_call(
        step_kernel,
        out_shape=(
            jax.ShapeDtypeStruct((1, 1, PAIRS, H), BF16),
            jax.ShapeDtypeStruct((1, 8, K * C), F32),
            jax.ShapeDtypeStruct((1, H // NGRP, E), F32),
            jax.ShapeDtypeStruct((1, 1), F32),
        ),
        in_specs=[smem] * 3 + [anywhere] * 9,
        out_specs=(anywhere, vmem, vmem, vmem),
        scratch_shapes=[
            pltpu.VMEM((OWN * NSEQ, SPAN), F32),
            pltpu.VMEM(conv_weight.shape, BF16),
            pltpu.VMEM(proj_weight.shape, BF16),
            *[pltpu.VMEM(t.shape, t.dtype) for t in tables],
            pltpu.VMEM((NSEQ * OWN * 16, 128), F32),
            pltpu.VMEM((NSEQ, OWN * 16, 128), F32),
            pltpu.VMEM((128, 128), F32),
            pltpu.VMEM(main, BF16),
            pltpu.VMEM(edge, F32),
            pltpu.VMEM(main, BF16),
            pltpu.VMEM(edge, F32),
            pltpu.VMEM((sources, 2, 16, 128), BF16),
            pltpu.VMEM((sources, OWN, 256), F32),
            pltpu.VMEM((8 * 2 * C, 128), F32),
            pltpu.VMEM((2 * C, 128), F32),
            pltpu.VMEM((2 * C, 256 + PAIRS), F32),
            pltpu.VMEM((16 + PAIRS, 128), F32),
            pltpu.VMEM((16 + PAIRS, 128), F32),
            pltpu.VMEM((PIECES, 2 * ROWS, K * C), BF16),
            pltpu.VMEM((K * C, SPAN), BF16),
            pltpu.VMEM((2, PAIRS, HB), BF16),
            pltpu.VMEM((BANDS, 8, HB), F32),
            pltpu.VMEM((K * C, HB), F32),
            pltpu.VMEM((1, H), F32),
            pltpu.VMEM((NSEQ, 1, H), F32),
            pltpu.VMEM((NGRP, 1, 2 * E), F32),
            pltpu.VMEM((NGRP, 1, 2 * E), F32),
            pltpu.VMEM((NGRP, 1, 2 * E), F32),
            pltpu.VMEM((NGRP, 2 * E), F32),
            pltpu.VMEM((NGRP, 2 * E), F32),
            pltpu.VMEM((H, E), F32),
            pltpu.VMEM((BANDS, 2, CHIPS, 16, K * C), F32),
            pltpu.VMEM(part, F32),
            pltpu.VMEM(part, F32),
            pltpu.VMEM(part, F32),
            pltpu.VMEM((NGRP, 8, K * C), F32),
            pltpu.VMEM((NGRP, 8, K * C), F32),
            dma((9,)), dma((2,)),
            dma((NSEQ,)), dma((NSEQ,)),
            dma((sources,)), dma((sources,)), dma((sources,)), dma((sources,)),
            dma((NSEQ,)), dma((NSEQ,)),
            dma((NGRP,)), dma((NGRP,)),
            dma((NGRP,)), dma((NGRP,)),
            dma((BANDS,)), dma((BANDS,)),
            dma((BANDS, CHIPS)), dma((BANDS, CHIPS)),
            dma((NGRP,)), dma((NGRP,)),
        ],
        compiler_params=pltpu.CompilerParams(
            collective_id=0, has_side_effects=True, vmem_limit_bytes=48 * 1024 * 1024),
        name="step",
    )(*[
        pltpu.with_memory_space_constraint(x, pltpu.HBM)
        for x in (positives, time_blocks, freq_blocks, series[0].T, conv_weight, proj_weight, *tables)
    ])
    return (encoded, loss[0, 0], conv_share, proj_share)


def solution(mesh):
    in_specs = (
        P("grp", "seq", "pair"),
        P("grp", None),
        P("grp", None),
        P(),
        P("pair", None, None),
        P("pair", None, None),
    )
    out_specs = (
        P("pair", "grp", "seq", None),
        P(),
        P("pair", ("grp", "seq"), None),
        P("pair", "grp", None),
    )
    return jax.shard_map(body, mesh=mesh, in_specs=in_specs, out_specs=out_specs, check_vma=False)
```

```python
import functools
import math

import jax
import jax.numpy as jnp
import numpy as np
from jax import lax
from jax.experimental import pallas as pl
from jax.experimental.pallas import tpu as pltpu
from jax.sharding import PartitionSpec as P

MESH = pl.DeviceIdType.MESH
F32 = jnp.float32
BF16 = jnp.bfloat16
HIGHEST = lax.Precision.HIGHEST

C = 64
H = 1024
E = 128
K = 8
SEQLEN = 32768
NSEQ = 16
NGRP = 8
NPAIR = 2
OWN = 2
SPAN = SEQLEN // NSEQ
PAIRS = SPAN // 2
BLOCKS = SPAN // 256
TAU = 0.2
LOSS_SCALE = 256.0
GELU_A = math.sqrt(2.0 / math.pi)
GELU_B = 0.044715 * GELU_A
CHIPS = NSEQ // 2
HB = 256
BANDS = H // HB
ROWS = 128
PIECES = PAIRS // ROWS
FLAT_FROM = 3.4
STRIP = 16
DEPTH = 2


def split(values):
    high = values.astype(np.float32).astype(BF16)
    low = (values - high.astype(np.float64)).astype(np.float32).astype(BF16)
    return high, low


def transform_tables():
    row = np.arange(256)
    a = (row // 16) * 16 + 2 * (row % 8) + (row % 16) // 8
    col = np.arange(256)
    k1 = 2 * (col % 128) + col // 128
    first = 2 * np.pi * ((a[:, None] * k1[None, :]) % 256) / 256
    first = np.concatenate([np.cos(first), -np.sin(first)], axis=1)
    b = np.arange(128)
    turn = 2 * np.pi * (b[:, None] * k1[None, :]) / SEQLEN
    turn = np.concatenate([np.cos(turn), np.sin(turn)], axis=1).astype(np.float32)
    k2 = np.arange(128)
    second = 2 * np.pi * ((k2[:, None] * b[None, :]) % 128) / 128
    cos, sin = np.cos(second), np.sin(second)
    second = np.block([[cos, sin], [-sin, cos]])
    pick = np.zeros((2, 128, 256), np.float32)
    for odd_row in range(2):
        for step in range(128):
            pick[odd_row, step, 128 * (step % 2) + 64 * odd_row + step // 2] = 1.0
    return (*split(first), turn, np.concatenate(split(second), axis=0), pick.astype(BF16))


def halves(values):
    high = values.astype(BF16)
    return high, (values - high.astype(F32)).astype(BF16)


def mul(a, b):
    return jnp.dot(a, b, preferred_element_type=F32)


def step_kernel(
    positives_in, time_blocks_in, freq_blocks_in, series_in, weight_in, proj_in,
    first_h_in, first_l_in, turn_in, second_in, pick_in,
    encoded, conv_out, proj_out, loss_out,
    positives, time_blocks, freq_blocks, raw, weight, proj, first_h, first_l, turn, second, pick,
    send, series, rows, time_main, time_halo, freq_main, freq_halo, feat, halo,
    tall, edges, wide, turned, across, patches, patches_t, held, total, grad_t,
    own_sum, all_sums, notes, own_notes, other_notes, own_rows, other_rows, table,
    grads, core_in, passed, chip_in, ready, grp_in,
    s_in, s_enc, s1, r1, s2, r2, s3, r3,
    s_sum, r_sum, s_own, r_own, s_oth, r_oth, s_core, r_core, s_chip, r_chip, s_grp, r_grp,
):
    me = lax.axis_index("seq")
    branch = lax.axis_index("pair")
    grp = lax.axis_index("grp")
    other = 1 - branch
    chip, core = me // 2, lax.rem(me, 2)
    sibling = me + 1 - 2 * core
    is_time = branch == 0

    loads = [
        pltpu.make_async_copy(src, dst, s_in.at[n])
        for n, (src, dst) in enumerate((
            (series_in, raw), (pick_in, pick), (first_h_in, first_h), (first_l_in, first_l),
            (turn_in, turn), (second_in, second),
            *[(weight_in.at[0, :, 128 * j:128 * (j + 1)], weight.at[j]) for j in range(K // 2)],
            (proj_in.at[0], proj), (positives_in, positives), (time_blocks_in, time_blocks),
            (freq_blocks_in, freq_blocks)))
    ]
    loads[0].start()

    barrier = pltpu.get_barrier_semaphore()

    def greet_seq(i, _):
        peer = lax.rem(me + i, NSEQ)

        @pl.when(i > 0)
        def _():
            pl.semaphore_signal(barrier, 1, device_id={"seq": peer}, device_id_type=MESH)

        pl.semaphore_signal(barrier, 1, device_id={"pair": other, "seq": peer}, device_id_type=MESH)
        return 0

    def greet_grp(i, _):
        peer = lax.rem(grp + i, NGRP)
        pl.semaphore_signal(barrier, 1, device_id={"grp": peer}, device_id_type=MESH)
        pl.semaphore_signal(barrier, 1, device_id={"pair": other, "grp": peer}, device_id_type=MESH)
        return 0

    lax.fori_loop(0, NSEQ, greet_seq, 0)
    lax.fori_loop(1, NGRP, greet_grp, 0)
    for load in loads[1:]:
        load.start()

    loads[0].wait()
    for q in range(BLOCKS):
        for odd in range(2):
            at = 128 * (2 * q + odd)
            send[pl.ds(8 * odd + q, NSEQ * OWN, stride=16), :] = raw[:, at:at + 128]
    pl.semaphore_wait(barrier, 2 * NSEQ - 1 + 2 * (NGRP - 1))

    def series_copy(i, dst):
        peer = lax.rem(me + i, NSEQ)
        return pltpu.make_async_remote_copy(
            src_ref=send.at[pl.ds(pl.multiple_of(32 * peer, 32), 32)], dst_ref=series.at[dst],
            send_sem=s1.at[i], recv_sem=r1.at[i], device_id={"seq": peer}, device_id_type=MESH)

    def start_series(i, _):
        series_copy(i, me).start()
        return 0

    lax.fori_loop(1, NSEQ, start_series, 0)
    series[me] = send[pl.ds(pl.multiple_of(32 * me, 32), 32), :]
    for load in loads[1:]:
        load.wait()
    table[...] = proj[pl.ds(pl.multiple_of(128 * grp, 128), 128), :].astype(F32)

    def wait_series(i, _):
        series_copy(i, lax.rem(me - i + NSEQ, NSEQ)).wait_recv()
        return 0

    lax.fori_loop(1, NSEQ, wait_series, 0)

    lane = lax.broadcasted_iota(jnp.int32, (NSEQ, 128), 1)

    def pack(values, main, edge):
        parts = [v.reshape(NSEQ, BLOCKS, 256) for v in values]
        block = jnp.concatenate(parts, axis=1).astype(BF16)
        main[:, 0] = block[:, :, :128]
        main[:, 1] = block[:, :, 128:]
        for c in range(OWN):
            for half in range(2):
                columns = slice(128 * half, 128 * (half + 1))
                rows[...] = values[c][:, columns]
                low = rows[pl.ds(0, NSEQ, stride=BLOCKS), :]
                high = rows[pl.ds(BLOCKS - 1, NSEQ, stride=BLOCKS), :]
                before = pltpu.roll(high, 1, 0)
                after = pltpu.roll(low, NSEQ - 1, 0)
                both = jnp.where(lane >= 64, before, after)
                for d in range(NSEQ):
                    edge[d, c:c + 1, columns] = both[d:d + 1]

    def view_copies(view, i, main, edge, slot):
        peer = lax.rem(me + i, NSEQ)
        target = {"pair": view, "seq": peer}
        n = view * NSEQ + i
        return (
            pltpu.make_async_remote_copy(
                src_ref=main.at[peer], dst_ref=feat.at[slot], send_sem=s2.at[n],
                recv_sem=r2.at[branch * NSEQ + i], device_id=target, device_id_type=MESH),
            pltpu.make_async_remote_copy(
                src_ref=edge.at[peer], dst_ref=halo.at[slot], send_sem=s3.at[n],
                recv_sem=r3.at[branch * NSEQ + i], device_id=target, device_id_type=MESH),
        )

    mine = branch * NSEQ + me

    def start_view(view, main, edge):
        def step(i, _):
            @pl.when(jnp.logical_or(i > 0, branch != view))
            def _():
                for copy in view_copies(view, i, main, edge, mine):
                    copy.start()
            return 0

        lax.fori_loop(0, NSEQ, step, 0)

        @pl.when(branch == view)
        def _():
            feat[mine] = main[me]
            halo[mine] = edge[me]

    flats = []
    for c in range(OWN):
        whole = series[:, 16 * c:16 * c + 16, :].reshape(256, 128)
        flats.append(jnp.concatenate([whole[:128].T, whole[128:].T], axis=1))
    high, low = halves(jnp.concatenate(flats, axis=0))
    part = mul(high, first_h[...]) + (mul(high, first_l[...]) + mul(low, first_h[...]))
    re, im = part[:, :256], part[:, 256:]
    cos = jnp.concatenate([turn[:, :256]] * OWN, axis=0)
    sin = jnp.concatenate([turn[:, 256:]] * OWN, axis=0)
    spun_re, spun_im = re * cos + im * sin, im * cos - re * sin
    powers = []
    for c in range(OWN):
        at = slice(128 * c, 128 * (c + 1))
        high, low = halves(jnp.concatenate([spun_re[at], spun_im[at]], axis=0))
        both = mul(second[...], high)
        spec = both[:256] + (both[256:] + mul(second[:256, :], low))
        re, im = spec[:128], spec[128:]
        powers.append(jnp.sqrt(1.0 + (re * re + im * im) * (1.0 / SEQLEN)))
    pack(powers, freq_main, freq_halo)
    start_view(1, freq_main, freq_halo)

    even = [series[:, 16 * c:16 * c + 8, :].reshape(128, 128) for c in range(OWN)]
    odd = [series[:, 16 * c + 8:16 * c + 16, :].reshape(128, 128) for c in range(OWN)]
    views = [
        jnp.dot(even[c].astype(BF16), pick[0], preferred_element_type=F32)
        + jnp.dot(odd[c].astype(BF16), pick[1], preferred_element_type=F32)
        for c in range(OWN)
    ]
    pack(views, time_main, time_halo)
    start_view(0, time_main, time_halo)

    def wait_view(i, _):
        peer = lax.rem(me - i + NSEQ, NSEQ)

        def arrivals(source):
            slot = source * NSEQ + peer
            target = {"pair": source, "seq": peer}
            return (
                pltpu.make_async_remote_copy(
                    src_ref=freq_main.at[peer], dst_ref=feat.at[slot], send_sem=s2.at[i],
                    recv_sem=r2.at[source * NSEQ + i], device_id=target, device_id_type=MESH),
                pltpu.make_async_remote_copy(
                    src_ref=freq_halo.at[peer], dst_ref=halo.at[slot], send_sem=s3.at[i],
                    recv_sem=r3.at[source * NSEQ + i], device_id=target, device_id_type=MESH),
            )

        @pl.when(i > 0)
        def _():
            for copy in arrivals(branch):
                copy.wait_recv()

        for copy in arrivals(other):
            copy.wait_recv()
        return 0

    lax.fori_loop(0, NSEQ, wait_view, 0)

    listed = [jnp.where(is_time, time_blocks[0, n], freq_blocks[0, n]) for n in range(16)]

    def keep(q):
        block = me * BLOCKS + q
        hit = listed[0] == block
        for n in range(1, 16):
            hit = jnp.logical_or(hit, listed[n] == block)
        drop = jnp.logical_or(hit, jnp.logical_or(block < 0, block >= NSEQ * BLOCKS))
        return jnp.where(drop, 0.0, 1.0).astype(F32)

    for parity in range(2):
        tall[parity * 512:(parity + 1) * 512, :] = feat[:, parity].astype(F32).reshape(512, 128)
        for source in range(NPAIR * NSEQ):
            edges[parity * C + OWN * source:parity * C + OWN * (source + 1), :] = (
                halo[source, :, parity * 128:(parity + 1) * 128])
    side = lax.broadcasted_iota(jnp.int32, (128, 128), 1)
    rim = edges[...].astype(BF16).astype(F32) * jnp.where(side >= 64, keep(-1), keep(BLOCKS))
    wide[:, 0:128] = rim
    wide[:, 128 + PAIRS:256 + PAIRS] = rim
    rim_t = rim.T
    turned[0:8, :] = rim_t[120:128]
    turned[8 + PAIRS:16 + PAIRS, :] = rim_t[0:8]
    for q in range(BLOCKS):
        piece = tall[pl.ds(q, 128, stride=BLOCKS), :] * keep(q)
        wide[:, 128 * (q + 1):128 * (q + 2)] = piece
        turned[8 + 128 * q:8 + 128 * (q + 1), :] = piece.T
    across[...] = pltpu.roll(turned[...], 64, 1)
    low_half = lax.broadcasted_iota(jnp.int32, (ROWS, 128), 1) < 64
    for j in range(K // 2):
        for r in range(PIECES):
            at = 8 + j - 2 + ROWS * r
            patches[r, j, 0:ROWS, :] = turned[at:at + ROWS, :].astype(BF16)
            patches[r, j, ROWS:2 * ROWS, :] = jnp.where(
                low_half, across[at:at + ROWS, :], across[at + 1:at + 1 + ROWS, :]).astype(BF16)
    for d in range(-2, 3):
        whole = wide[...]
        if d != 0:
            whole = pltpu.roll(whole, (-d) % (256 + PAIRS), 1)
        part = whole[:, 128:128 + PAIRS].astype(BF16)
        j = d + 2
        for r in range(PIECES):
            chunk = part[:, ROWS * r:ROWS * (r + 1)]
            if j < K // 2:
                patches_t[2 * r, 128 * j:128 * (j + 1), :] = chunk
                patches_t[2 * r + 1, 128 * j:128 * j + 64, :] = chunk[64:]
            if j > 0:
                patches_t[2 * r + 1, 128 * (j - 1) + 64:128 * j, :] = chunk[:64]

    def encoded_copies(n):
        slot = lax.rem(n, 2)
        return [
            pltpu.make_async_copy(
                held.at[slot, k],
                encoded.at[0, 0, :, pl.ds(pl.multiple_of(n * HB + 128 * k, 128), 128)],
                s_enc.at[slot, k])
            for k in range(HB // 128)
        ]

    def core_copy(n):
        return pltpu.make_async_remote_copy(
            src_ref=grads.at[n, 1 - core], dst_ref=core_in.at[n], send_sem=s_core.at[n],
            recv_sem=r_core.at[n], device_id={"seq": sibling}, device_id_type=MESH)

    def chip_copy(n, i, slot):
        j = lax.rem(chip + i, CHIPS)
        return pltpu.make_async_remote_copy(
            src_ref=passed.at[n, j], dst_ref=chip_in.at[n, slot], send_sem=s_chip.at[n, i],
            recv_sem=r_chip.at[n, i], device_id={"seq": 2 * j + core}, device_id_type=MESH)

    def sum_copy(i, slot):
        return pltpu.make_async_remote_copy(
            src_ref=own_sum, dst_ref=all_sums.at[slot], send_sem=s_sum.at[i],
            recv_sem=r_sum.at[i], device_id={"seq": lax.rem(me + i, NSEQ)}, device_id_type=MESH)

    def pass_on(n):
        core_copy(n).wait_recv()

        def one(i, _):
            j = lax.rem(chip + i, CHIPS)
            passed[n, j] = grads[n, core, j] + core_in[n, j]
            chip_copy(n, i, chip).start()
            return 0

        lax.fori_loop(1, CHIPS, one, 0)

    def forward(n, _):
        at = pl.ds(pl.multiple_of(n * HB, HB), HB)
        weights = jnp.concatenate([weight[j, at, :] for j in range(K // 2)], axis=1)

        @pl.when(n >= 2)
        def _():
            for copy in encoded_copies(n):
                copy.wait()

        slot = lax.rem(n, 2)

        def product(r):
            rows = jnp.concatenate([patches[r, j] for j in range(K // 2)], axis=1)
            return lax.dot_general(
                rows, weights, (((1,), (1,)), ((), ())), preferred_element_type=F32)

        counts = [jnp.zeros((8, HB), F32)] * 3
        kept = []
        preact = product(0)
        for r in range(PIECES):
            following = product(r + 1) if r + 1 < PIECES else None
            firsts, seconds = [], []
            for q in range(0, ROWS, STRIP):
                slopes, active, flat = [], [], []
                for base in (0, ROWS):
                    value = preact[base + q:base + q + STRIP]
                    square = value * value
                    inner = value * (GELU_A + GELU_B * square)
                    half = 0.5 * jnp.tanh(inner)
                    gate = 0.5 + half
                    active.append(value * gate)
                    slopes.append(gate + active[-1] * (
                        (0.5 - half) * (2.0 * GELU_A + (6.0 * GELU_B) * square)))
                    flat.append(jnp.where(value > FLAT_FROM, 1.0, 0.0))
                pair = active[0] + active[1]
                mean = (pair * 0.5).astype(BF16)
                for k in range(HB // 128):
                    held[slot, k, r * ROWS + q:r * ROWS + q + STRIP, :] = (
                        mean[:, 128 * k:128 * (k + 1)])
                for k, both in enumerate((pair, flat[0] + flat[1], slopes[0] + slopes[1])):
                    counts[k] = counts[k] + jnp.sum(both.reshape(STRIP // 8, 8, HB), axis=0)
                firsts.append(slopes[0].astype(BF16))
                seconds.append(slopes[1].astype(BF16))
            kept.extend(firsts + seconds)
            if (r + 1) % DEPTH == 0:
                columns = range(2 * (r + 1 - DEPTH), 2 * (r + 1))
                update = mul(
                    jnp.concatenate([patches_t[k] for k in columns], axis=1),
                    jnp.concatenate(kept, axis=0))
                if r + 1 == DEPTH:
                    grad_t[...] = update
                else:
                    grad_t[...] += update
                kept = []
            preact = following
        for k in range(3):
            total[n, k] = counts[k]
        for copy in encoded_copies(n):
            copy.start()

        @pl.when(n == BANDS - 1)
        def _():
            for band in range(BANDS):
                for k in range(3):
                    at = H * k + HB * band
                    own_sum[:, at:at + HB] = jnp.sum(total[band, k], axis=0, keepdims=True)

            def start_sum(i, _):
                sum_copy(i, me).start()
                return 0

            lax.fori_loop(1, NSEQ, start_sum, 0)
            all_sums[me] = own_sum[...]

        grad = grad_t[...].T.reshape(2, CHIPS, 2, 8, K * C)
        for e in range(2):
            grads[n, e, :, 0:8, :] = grad[0, :, e]
            grads[n, e, :, 8:16, :] = grad[1, :, e]
        core_copy(n).start()

        @pl.when(n >= 1)
        def _():
            pass_on(n - 1)

        return 0

    lax.fori_loop(0, BANDS, forward, 0)

    def wait_sum(i, _):
        sum_copy(i, lax.rem(me - i + NSEQ, NSEQ)).wait_recv()
        return 0

    lax.fori_loop(1, NSEQ, wait_sum, 0)
    sums = jnp.sum(all_sums[...], axis=0)
    pooled = sums[:, :H] * (1.0 / SEQLEN)
    share = jnp.minimum(sums[:, H:2 * H] / jnp.maximum(sums[:, 2 * H:], 1.0), 1.0)
    left, thirds = pooled, []
    for _ in range(3):
        thirds.append(left.astype(BF16).astype(F32))
        left = left - thirds[-1]
    thirds = jnp.concatenate(thirds + [jnp.zeros((5, H), F32)], axis=0).astype(BF16)
    latent = jnp.sum(mul(thirds, proj[...]), axis=0, keepdims=True)
    for g in range(NGRP):
        at = slice(128 * g, 128 * (g + 1))
        notes[g] = jnp.concatenate([latent, pooled[:, at], share[:, at]], axis=1)

    def own_copy(i, slot):
        peer = lax.rem(grp + i, NGRP)
        return pltpu.make_async_remote_copy(
            src_ref=notes.at[peer], dst_ref=own_notes.at[slot], send_sem=s_own.at[i],
            recv_sem=r_own.at[i], device_id={"grp": peer}, device_id_type=MESH)

    def other_copy(i, slot):
        peer = lax.rem(grp + i, NGRP)
        return pltpu.make_async_remote_copy(
            src_ref=notes.at[peer], dst_ref=other_notes.at[slot], send_sem=s_oth.at[i],
            recv_sem=r_oth.at[i], device_id={"pair": other, "grp": peer}, device_id_type=MESH)

    def start_notes(i, _):
        @pl.when(i > 0)
        def _():
            own_copy(i, grp).start()

        other_copy(i, grp).start()
        return 0

    lax.fori_loop(0, NGRP, start_notes, 0)
    own_notes[grp] = notes[grp]
    pass_on(BANDS - 1)

    def wait_chip(i, _):
        for n in range(BANDS):
            chip_copy(n, i, lax.rem(chip - i + CHIPS, CHIPS)).wait_recv()
        return 0

    lax.fori_loop(1, CHIPS, wait_chip, 0)
    for n in range(BANDS):
        chip_in[n, chip] = grads[n, core, chip] + core_in[n, chip]
        whole = chip_in[n, 0]
        for j in range(1, CHIPS):
            whole = whole + chip_in[n, j]
        for k in range(2):
            g = 2 * n + k
            ready[g] = whole[8 * k:8 * (k + 1)]

    def grp_copy(i, slot):
        peer = lax.rem(grp + i, NGRP)
        return pltpu.make_async_remote_copy(
            src_ref=ready.at[peer], dst_ref=grp_in.at[slot], send_sem=s_grp.at[i],
            recv_sem=r_grp.at[i], device_id={"grp": peer}, device_id_type=MESH)

    def start_grp(i, _):
        grp_copy(i, grp).start()
        return 0

    lax.fori_loop(1, NGRP, start_grp, 0)
    grp_in[grp] = ready[grp]

    def wait_notes(i, _):
        source = lax.rem(grp - i + NGRP, NGRP)

        @pl.when(i > 0)
        def _():
            own_copy(i, source).wait_recv()

        other_copy(i, source).wait_recv()
        return 0

    lax.fori_loop(0, NGRP, wait_notes, 0)
    for g in range(NGRP):
        own_rows[g:g + 1, :] = own_notes[g]
        other_rows[g:g + 1, :] = other_notes[g]
    z_own, z_other = own_rows[:, :E], other_rows[:, :E]
    scale = lax.rsqrt(jnp.sum(z_own * z_own, axis=1, keepdims=True) + 1e-06)
    scale_other = lax.rsqrt(jnp.sum(z_other * z_other, axis=1, keepdims=True) + 1e-06)
    e_own, e_other = z_own * scale, z_other * scale_other
    time_emb = jnp.where(is_time, e_own, e_other)
    freq_emb = jnp.where(is_time, e_other, e_own)
    dot = functools.partial(lax.dot_general, precision=HIGHEST, preferred_element_type=F32)
    logits = dot(time_emb, freq_emb, (((1,), (1,)), ((), ()))) * (1.0 / TAU)
    row = lax.broadcasted_iota(jnp.int32, (NGRP, NGRP), 0)
    col = lax.broadcasted_iota(jnp.int32, (NGRP, NGRP), 1)
    target = jnp.zeros((NGRP, NGRP), F32)
    for i in range(NGRP):
        target = jnp.where(jnp.logical_and(row == i, col == positives[i]), 1.0, target)
    exponent = jnp.exp(logits)
    by_row = jnp.sum(exponent, axis=1, keepdims=True)
    by_col = jnp.sum(exponent, axis=0, keepdims=True)
    slope = (exponent / by_row + exponent / by_col - 2.0 * target) * (
        LOSS_SCALE / (TAU * 2 * NGRP))
    d_time = dot(slope, freq_emb, (((1,), (0,)), ((), ())))
    d_freq = dot(slope, time_emb, (((0,), (0,)), ((), ())))
    d_emb = jnp.where(is_time, d_time, d_freq)
    along = jnp.sum(z_own * d_emb, axis=1, keepdims=True)
    d_latent = scale * d_emb - z_own * (scale * scale * scale * along)
    own_proj = table[pl.ds(pl.multiple_of(8 * me, 8), 8), :] * (1.0 / SEQLEN)
    take = jnp.where(
        lax.broadcasted_iota(jnp.int32, (8, 128), 1)
        == 8 * me + lax.broadcasted_iota(jnp.int32, (8, 128), 0), 1.0, 0.0)
    shares = dot(take, own_rows[:, 2 * E:], (((1,), (1,)), ((), ())))
    exact = jnp.concatenate([
        jnp.sum(own_proj * d_latent[g:g + 1], axis=1, keepdims=True) for g in range(NGRP)], axis=1)
    blend = exact + shares * (exact.astype(BF16).astype(F32) - exact)
    factors = [blend[:, g:g + 1] for g in range(NGRP)]

    picked = jnp.sum(jnp.sum(target * logits, axis=1, keepdims=True), axis=0, keepdims=True)
    lse = jnp.sum(jnp.log(by_row), axis=0, keepdims=True) + jnp.sum(
        jnp.log(by_col), axis=1, keepdims=True)
    loss_out[...] = (lse - 2.0 * picked) * (1.0 / (2 * NGRP))
    proj_out[0] = dot(own_rows[:, E:2 * E], d_latent, (((0,), (0,)), ((), ())))
    def wait_grp(i, _):
        grp_copy(i, lax.rem(grp - i + NGRP, NGRP)).wait_recv()
        return 0

    lax.fori_loop(1, NGRP, wait_grp, 0)
    result = grp_in[0] * factors[0]
    for g in range(1, NGRP):
        result = result + grp_in[g] * factors[g]
    conv_out[0] = result
    for n in range(BANDS - 2, BANDS):
        for copy in encoded_copies(n):
            copy.wait()

    def sent_seq(i, _):
        for view, main, edge in ((0, time_main, time_halo), (1, freq_main, freq_halo)):
            @pl.when(jnp.logical_or(i > 0, branch != view))
            def _():
                for copy in view_copies(view, i, main, edge, mine):
                    copy.wait_send()

        @pl.when(i > 0)
        def _():
            series_copy(i, me).wait_send()
            sum_copy(i, me).wait_send()
        return 0

    def sent_grp(i, _):
        @pl.when(i > 0)
        def _():
            for n in range(BANDS):
                chip_copy(n, i, chip).wait_send()
            own_copy(i, grp).wait_send()
            grp_copy(i, grp).wait_send()

        other_copy(i, grp).wait_send()
        return 0

    lax.fori_loop(0, NSEQ, sent_seq, 0)
    for n in range(BANDS):
        core_copy(n).wait_send()

    lax.fori_loop(0, CHIPS, sent_grp, 0)


def finish_kernel(*refs):
    sems = refs[8]
    copies = [pltpu.make_async_copy(refs[n], refs[4 + n], sems.at[n]) for n in range(4)]
    for copy in copies:
        copy.start()
    for copy in copies:
        copy.wait()


def body(series, time_blocks, freq_blocks, positives, conv_weight, proj_weight):
    vmem = pl.BlockSpec(memory_space=pltpu.VMEM)
    hbm = pl.BlockSpec(memory_space=pltpu.HBM)
    anywhere = pl.BlockSpec(memory_space=pl.ANY)
    tables = [jnp.asarray(t) for t in transform_tables()]
    sources = NPAIR * NSEQ
    dma = pltpu.SemaphoreType.DMA
    part = (BANDS, CHIPS, 16, K * C)
    main, edge = (NSEQ, 2, 16, 128), (NSEQ, OWN, 256)
    encoded, conv_share, proj_share, loss = pl.pallas_call(
        step_kernel,
        out_shape=(
            jax.ShapeDtypeStruct((1, 1, PAIRS, H), BF16),
            jax.ShapeDtypeStruct((1, 8, K * C), F32),
            jax.ShapeDtypeStruct((1, H // NGRP, E), F32),
            jax.ShapeDtypeStruct((1, 1), F32),
        ),
        in_specs=[hbm] * 11,
        out_specs=(anywhere, vmem, vmem, vmem),
        scratch_shapes=[
            pltpu.SMEM((NGRP,), jnp.int32),
            pltpu.SMEM((1, 16), jnp.int32),
            pltpu.SMEM((1, 16), jnp.int32),
            pltpu.VMEM((OWN * NSEQ, SPAN), F32),
            pltpu.VMEM((K // 2, H, 128), BF16),
            pltpu.VMEM((H, E), BF16),
            *[pltpu.VMEM(t.shape, t.dtype) for t in tables],
            pltpu.VMEM((NSEQ * OWN * 16, 128), F32),
            pltpu.VMEM((NSEQ, OWN * 16, 128), F32),
            pltpu.VMEM((128, 128), F32),
            pltpu.VMEM(main, BF16),
            pltpu.VMEM(edge, F32),
            pltpu.VMEM(main, BF16),
            pltpu.VMEM(edge, F32),
            pltpu.VMEM((sources, 2, 16, 128), BF16),
            pltpu.VMEM((sources, OWN, 256), F32),
            pltpu.VMEM((8 * 2 * C, 128), F32),
            pltpu.VMEM((2 * C, 128), F32),
            pltpu.VMEM((2 * C, 256 + PAIRS), F32),
            pltpu.VMEM((16 + PAIRS, 128), F32),
            pltpu.VMEM((16 + PAIRS, 128), F32),
            pltpu.VMEM((PIECES, K // 2, 2 * ROWS, 128), BF16),
            pltpu.VMEM((2 * PIECES, K * C, 128), BF16),
            pltpu.VMEM((2, HB // 128, PAIRS, 128), BF16),
            pltpu.VMEM((BANDS, 3, 8, HB), F32),
            pltpu.VMEM((K * C, HB), F32),
            pltpu.VMEM((1, 3 * H), F32),
            pltpu.VMEM((NSEQ, 1, 3 * H), F32),
            pltpu.VMEM((NGRP, 1, 3 * E), F32),
            pltpu.VMEM((NGRP, 1, 3 * E), F32),
            pltpu.VMEM((NGRP, 1, 3 * E), F32),
            pltpu.VMEM((NGRP, 3 * E), F32),
            pltpu.VMEM((NGRP, 3 * E), F32),
            pltpu.VMEM((128, E), F32),
            pltpu.VMEM((BANDS, 2, CHIPS, 16, K * C), F32),
            pltpu.VMEM(part, F32),
            pltpu.VMEM(part, F32),
            pltpu.VMEM(part, F32),
            pltpu.VMEM((NGRP, 8, K * C), F32),
            pltpu.VMEM((NGRP, 8, K * C), F32),
            dma((14,)), dma((2, 2)),
            dma((NSEQ,)), dma((NSEQ,)),
            dma((sources,)), dma((sources,)), dma((sources,)), dma((sources,)),
            dma((NSEQ,)), dma((NSEQ,)),
            dma((NGRP,)), dma((NGRP,)),
            dma((NGRP,)), dma((NGRP,)),
            dma((BANDS,)), dma((BANDS,)),
            dma((BANDS, CHIPS)), dma((BANDS, CHIPS)),
            dma((NGRP,)), dma((NGRP,)),
        ],
        compiler_params=pltpu.CompilerParams(
            collective_id=0, has_side_effects=True, vmem_limit_bytes=48 * 1024 * 1024),
        name="step",
    )(*[
        pltpu.with_memory_space_constraint(x, pltpu.HBM)
        for x in (positives, time_blocks, freq_blocks, series[0].T, conv_weight, proj_weight, *tables)
    ])
    outs = [
        pltpu.with_memory_space_constraint(x, pltpu.VMEM)
        for x in (encoded, conv_share, proj_share, loss)
    ]
    encoded, conv_share, proj_share, loss = pl.pallas_call(
        finish_kernel,
        out_shape=[jax.ShapeDtypeStruct(x.shape, x.dtype) for x in outs],
        in_specs=[pl.BlockSpec(memory_space=pltpu.VMEM)] * 4,
        out_specs=[pl.BlockSpec(memory_space=pltpu.HBM)] * 4,
        scratch_shapes=[dma((4,))],
        name="finish",
    )(*outs)
    return (encoded, loss[0, 0], conv_share, proj_share)


def solution(mesh):
    in_specs = (
        P("grp", "seq", "pair"),
        P("grp", None),
        P("grp", None),
        P(),
        P("pair", None, None),
        P("pair", None, None),
    )
    out_specs = (
        P("pair", "grp", "seq", None),
        P(),
        P("pair", ("grp", "seq"), None),
        P("pair", "grp", None),
    )
    return jax.shard_map(body, mesh=mesh, in_specs=in_specs, out_specs=out_specs, check_vma=False)
```

```python
import functools
import math

import jax
import jax.numpy as jnp
import numpy as np
from jax import lax
from jax.experimental import pallas as pl
from jax.experimental.pallas import tpu as pltpu
from jax.sharding import PartitionSpec as P

MESH = pl.DeviceIdType.MESH
F32 = jnp.float32
BF16 = jnp.bfloat16
HIGHEST = lax.Precision.HIGHEST

C = 64
H = 1024
E = 128
K = 8
SEQLEN = 32768
NSEQ = 16
NGRP = 8
NPAIR = 2
OWN = 2
SPAN = SEQLEN // NSEQ
PAIRS = SPAN // 2
BLOCKS = SPAN // 256
TAU = 0.2
LOSS_SCALE = 256.0
GELU_A = math.sqrt(2.0 / math.pi)
GELU_B = 0.044715 * GELU_A
CHIPS = NSEQ // 2
HB = 256
BANDS = H // HB
ROWS = 128
PIECES = PAIRS // ROWS
FLAT_FROM = 3.4
STRIP = 16
DEPTH = 2


def split(values):
    high = values.astype(np.float32).astype(BF16)
    low = (values - high.astype(np.float64)).astype(np.float32).astype(BF16)
    return high, low


def transform_tables():
    row = np.arange(256)
    a = (row // 16) * 16 + 2 * (row % 8) + (row % 16) // 8
    col = np.arange(256)
    k1 = 2 * (col % 128) + col // 128
    first = 2 * np.pi * ((a[:, None] * k1[None, :]) % 256) / 256
    first = np.concatenate([np.cos(first), -np.sin(first)], axis=1)
    b = np.arange(128)
    turn = 2 * np.pi * (b[:, None] * k1[None, :]) / SEQLEN
    turn = np.concatenate([np.cos(turn), np.sin(turn)], axis=1).astype(np.float32)
    k2 = np.arange(128)
    second = 2 * np.pi * ((k2[:, None] * b[None, :]) % 128) / 128
    cos, sin = np.cos(second), np.sin(second)
    second = np.block([[cos, sin], [-sin, cos]])
    pick = np.zeros((2, 128, 256), np.float32)
    for odd_row in range(2):
        for step in range(128):
            pick[odd_row, step, 128 * (step % 2) + 64 * odd_row + step // 2] = 1.0
    return (*split(first), turn, np.concatenate(split(second), axis=0), pick.astype(BF16))


def halves(values):
    high = values.astype(BF16)
    return high, (values - high.astype(F32)).astype(BF16)


def mul(a, b):
    return jnp.dot(a, b, preferred_element_type=F32)


def step_kernel(
    positives_in, time_blocks_in, freq_blocks_in, series_in, weight_in, proj_in,
    first_h_in, first_l_in, turn_in, second_in, pick_in,
    encoded, conv_out, proj_out, loss_out,
    positives, time_blocks, freq_blocks, raw, weight, proj, first_h, first_l, turn, second, pick,
    send, series, rows, time_main, time_halo, freq_main, freq_halo, feat, halo,
    tall, edges, wide, turned, across, patches, patches_t, held, total, grad_t,
    own_sum, all_sums, notes, own_notes, other_notes, own_rows, other_rows, table,
    grads, core_in, passed, chip_in, ready, grp_in,
    s_in, s_enc, s1, r1, s2, r2, s3, r3,
    s_sum, r_sum, s_own, r_own, s_oth, r_oth, s_core, r_core, s_chip, r_chip, s_grp, r_grp,
):
    me = lax.axis_index("seq")
    branch = lax.axis_index("pair")
    grp = lax.axis_index("grp")
    other = 1 - branch
    chip, core = me // 2, lax.rem(me, 2)
    sibling = me + 1 - 2 * core
    is_time = branch == 0

    loads = [
        pltpu.make_async_copy(src, dst, s_in.at[n])
        for n, (src, dst) in enumerate((
            (series_in, raw), (pick_in, pick), (first_h_in, first_h), (first_l_in, first_l),
            (turn_in, turn), (second_in, second),
            *[(weight_in.at[0, :, 128 * j:128 * (j + 1)], weight.at[j]) for j in range(K // 2)],
            (proj_in.at[0], proj), (positives_in, positives), (time_blocks_in, time_blocks),
            (freq_blocks_in, freq_blocks)))
    ]
    loads[0].start()

    barrier = pltpu.get_barrier_semaphore()

    def greet_seq(i, _):
        peer = lax.rem(me + i, NSEQ)

        @pl.when(i > 0)
        def _():
            pl.semaphore_signal(barrier, 1, device_id={"seq": peer}, device_id_type=MESH)

        pl.semaphore_signal(barrier, 1, device_id={"pair": other, "seq": peer}, device_id_type=MESH)
        return 0

    def greet_grp(i, _):
        peer = lax.rem(grp + i, NGRP)
        pl.semaphore_signal(barrier, 1, device_id={"grp": peer}, device_id_type=MESH)
        pl.semaphore_signal(barrier, 1, device_id={"pair": other, "grp": peer}, device_id_type=MESH)
        return 0

    lax.fori_loop(0, NSEQ, greet_seq, 0)
    lax.fori_loop(1, NGRP, greet_grp, 0)
    for load in loads[1:]:
        load.start()

    loads[0].wait()
    for q in range(BLOCKS):
        for odd in range(2):
            at = 128 * (2 * q + odd)
            send[pl.ds(8 * odd + q, NSEQ * OWN, stride=16), :] = raw[:, at:at + 128]
    pl.semaphore_wait(barrier, 2 * NSEQ - 1 + 2 * (NGRP - 1))

    def series_copy(i, dst):
        peer = lax.rem(me + i, NSEQ)
        return pltpu.make_async_remote_copy(
            src_ref=send.at[pl.ds(pl.multiple_of(32 * peer, 32), 32)], dst_ref=series.at[dst],
            send_sem=s1.at[i], recv_sem=r1.at[i], device_id={"seq": peer}, device_id_type=MESH)

    def start_series(i, _):
        series_copy(i, me).start()
        return 0

    lax.fori_loop(1, NSEQ, start_series, 0)
    series[me] = send[pl.ds(pl.multiple_of(32 * me, 32), 32), :]
    for load in loads[1:]:
        load.wait()
    table[...] = proj[pl.ds(pl.multiple_of(128 * grp, 128), 128), :].astype(F32)

    def wait_series(i, _):
        series_copy(i, lax.rem(me - i + NSEQ, NSEQ)).wait_recv()
        return 0

    lax.fori_loop(1, NSEQ, wait_series, 0)

    lane = lax.broadcasted_iota(jnp.int32, (NSEQ, 128), 1)

    def pack(values, main, edge):
        parts = [v.reshape(NSEQ, BLOCKS, 256) for v in values]
        block = jnp.concatenate(parts, axis=1).astype(BF16)
        main[:, 0] = block[:, :, :128]
        main[:, 1] = block[:, :, 128:]
        for c in range(OWN):
            for half in range(2):
                columns = slice(128 * half, 128 * (half + 1))
                rows[...] = values[c][:, columns]
                low = rows[pl.ds(0, NSEQ, stride=BLOCKS), :]
                high = rows[pl.ds(BLOCKS - 1, NSEQ, stride=BLOCKS), :]
                before = pltpu.roll(high, 1, 0)
                after = pltpu.roll(low, NSEQ - 1, 0)
                both = jnp.where(lane >= 64, before, after)
                for d in range(NSEQ):
                    edge[d, c:c + 1, columns] = both[d:d + 1]

    def view_copies(view, i, main, edge, slot):
        peer = lax.rem(me + i, NSEQ)
        target = {"pair": view, "seq": peer}
        n = view * NSEQ + i
        return (
            pltpu.make_async_remote_copy(
                src_ref=main.at[peer], dst_ref=feat.at[slot], send_sem=s2.at[n],
                recv_sem=r2.at[branch * NSEQ + i], device_id=target, device_id_type=MESH),
            pltpu.make_async_remote_copy(
                src_ref=edge.at[peer], dst_ref=halo.at[slot], send_sem=s3.at[n],
                recv_sem=r3.at[branch * NSEQ + i], device_id=target, device_id_type=MESH),
        )

    mine = branch * NSEQ + me

    def start_view(view, main, edge):
        def step(i, _):
            @pl.when(jnp.logical_or(i > 0, branch != view))
            def _():
                for copy in view_copies(view, i, main, edge, mine):
                    copy.start()
            return 0

        lax.fori_loop(0, NSEQ, step, 0)

        @pl.when(branch == view)
        def _():
            feat[mine] = main[me]
            halo[mine] = edge[me]

    flats = []
    for c in range(OWN):
        whole = series[:, 16 * c:16 * c + 16, :].reshape(256, 128)
        flats.append(jnp.concatenate([whole[:128].T, whole[128:].T], axis=1))
    high, low = halves(jnp.concatenate(flats, axis=0))
    part = mul(high, first_h[...]) + (mul(high, first_l[...]) + mul(low, first_h[...]))
    re, im = part[:, :256], part[:, 256:]
    cos = jnp.concatenate([turn[:, :256]] * OWN, axis=0)
    sin = jnp.concatenate([turn[:, 256:]] * OWN, axis=0)
    spun_re, spun_im = re * cos + im * sin, im * cos - re * sin
    powers = []
    for c in range(OWN):
        at = slice(128 * c, 128 * (c + 1))
        high, low = halves(jnp.concatenate([spun_re[at], spun_im[at]], axis=0))
        both = mul(second[...], high)
        spec = both[:256] + (both[256:] + mul(second[:256, :], low))
        re, im = spec[:128], spec[128:]
        powers.append(jnp.sqrt(1.0 + (re * re + im * im) * (1.0 / SEQLEN)))
    pack(powers, freq_main, freq_halo)
    start_view(1, freq_main, freq_halo)

    even = [series[:, 16 * c:16 * c + 8, :].reshape(128, 128) for c in range(OWN)]
    odd = [series[:, 16 * c + 8:16 * c + 16, :].reshape(128, 128) for c in range(OWN)]
    views = [
        jnp.dot(even[c].astype(BF16), pick[0], preferred_element_type=F32)
        + jnp.dot(odd[c].astype(BF16), pick[1], preferred_element_type=F32)
        for c in range(OWN)
    ]
    pack(views, time_main, time_halo)
    start_view(0, time_main, time_halo)

    def wait_view(i, _):
        peer = lax.rem(me - i + NSEQ, NSEQ)

        def arrivals(source):
            slot = source * NSEQ + peer
            target = {"pair": source, "seq": peer}
            return (
                pltpu.make_async_remote_copy(
                    src_ref=freq_main.at[peer], dst_ref=feat.at[slot], send_sem=s2.at[i],
                    recv_sem=r2.at[source * NSEQ + i], device_id=target, device_id_type=MESH),
                pltpu.make_async_remote_copy(
                    src_ref=freq_halo.at[peer], dst_ref=halo.at[slot], send_sem=s3.at[i],
                    recv_sem=r3.at[source * NSEQ + i], device_id=target, device_id_type=MESH),
            )

        @pl.when(i > 0)
        def _():
            for copy in arrivals(branch):
                copy.wait_recv()

        for copy in arrivals(other):
            copy.wait_recv()
        return 0

    lax.fori_loop(0, NSEQ, wait_view, 0)

    listed = [jnp.where(is_time, time_blocks[0, n], freq_blocks[0, n]) for n in range(16)]

    def keep(q):
        block = me * BLOCKS + q
        hit = listed[0] == block
        for n in range(1, 16):
            hit = jnp.logical_or(hit, listed[n] == block)
        drop = jnp.logical_or(hit, jnp.logical_or(block < 0, block >= NSEQ * BLOCKS))
        return jnp.where(drop, 0.0, 1.0).astype(F32)

    for parity in range(2):
        tall[parity * 512:(parity + 1) * 512, :] = feat[:, parity].astype(F32).reshape(512, 128)
        for source in range(NPAIR * NSEQ):
            edges[parity * C + OWN * source:parity * C + OWN * (source + 1), :] = (
                halo[source, :, parity * 128:(parity + 1) * 128])
    side = lax.broadcasted_iota(jnp.int32, (128, 128), 1)
    rim = edges[...].astype(BF16).astype(F32) * jnp.where(side >= 64, keep(-1), keep(BLOCKS))
    wide[:, 0:128] = rim
    wide[:, 128 + PAIRS:256 + PAIRS] = rim
    rim_t = rim.T
    turned[0:8, :] = rim_t[120:128]
    turned[8 + PAIRS:16 + PAIRS, :] = rim_t[0:8]
    for q in range(BLOCKS):
        piece = tall[pl.ds(q, 128, stride=BLOCKS), :] * keep(q)
        wide[:, 128 * (q + 1):128 * (q + 2)] = piece
        turned[8 + 128 * q:8 + 128 * (q + 1), :] = piece.T
    across[...] = pltpu.roll(turned[...], 64, 1)
    low_half = lax.broadcasted_iota(jnp.int32, (ROWS, 128), 1) < 64
    for j in range(K // 2):
        for r in range(PIECES):
            at = 8 + j - 2 + ROWS * r
            patches[r, j, 0:ROWS, :] = turned[at:at + ROWS, :].astype(BF16)
            patches[r, j, ROWS:2 * ROWS, :] = jnp.where(
                low_half, across[at:at + ROWS, :], across[at + 1:at + 1 + ROWS, :]).astype(BF16)
    for d in range(-2, 3):
        whole = wide[...]
        if d != 0:
            whole = pltpu.roll(whole, (-d) % (256 + PAIRS), 1)
        part = whole[:, 128:128 + PAIRS].astype(BF16)
        j = d + 2
        for r in range(PIECES):
            chunk = part[:, ROWS * r:ROWS * (r + 1)]
            if j < K // 2:
                patches_t[2 * r, 128 * j:128 * (j + 1), :] = chunk
                patches_t[2 * r + 1, 128 * j:128 * j + 64, :] = chunk[64:]
            if j > 0:
                patches_t[2 * r + 1, 128 * (j - 1) + 64:128 * j, :] = chunk[:64]

    def encoded_copies(n):
        slot = lax.rem(n, 2)
        return [
            pltpu.make_async_copy(
                held.at[slot, k],
                encoded.at[0, 0, :, pl.ds(pl.multiple_of(n * HB + 128 * k, 128), 128)],
                s_enc.at[slot, k])
            for k in range(HB // 128)
        ]

    def core_copy(n):
        return pltpu.make_async_remote_copy(
            src_ref=grads.at[n, 1 - core], dst_ref=core_in.at[n], send_sem=s_core.at[n],
            recv_sem=r_core.at[n], device_id={"seq": sibling}, device_id_type=MESH)

    def chip_copy(n, i, slot):
        j = lax.rem(chip + i, CHIPS)
        return pltpu.make_async_remote_copy(
            src_ref=passed.at[n, j], dst_ref=chip_in.at[n, slot], send_sem=s_chip.at[n, i],
            recv_sem=r_chip.at[n, i], device_id={"seq": 2 * j + core}, device_id_type=MESH)

    def sum_copy(i, slot):
        return pltpu.make_async_remote_copy(
            src_ref=own_sum, dst_ref=all_sums.at[slot], send_sem=s_sum.at[i],
            recv_sem=r_sum.at[i], device_id={"seq": lax.rem(me + i, NSEQ)}, device_id_type=MESH)

    def pass_on(n):
        core_copy(n).wait_recv()

        def one(i, _):
            j = lax.rem(chip + i, CHIPS)
            passed[n, j] = grads[n, core, j] + core_in[n, j]
            chip_copy(n, i, chip).start()
            return 0

        lax.fori_loop(1, CHIPS, one, 0)

    def forward(n, _):
        at = pl.ds(pl.multiple_of(n * HB, HB), HB)
        weights = jnp.concatenate([weight[j, at, :] for j in range(K // 2)], axis=1)

        @pl.when(n >= 2)
        def _():
            for copy in encoded_copies(n):
                copy.wait()

        slot = lax.rem(n, 2)

        def product(r):
            rows = jnp.concatenate([patches[r, j] for j in range(K // 2)], axis=1)
            return lax.dot_general(
                rows, weights, (((1,), (1,)), ((), ())), preferred_element_type=F32)

        counts = [jnp.zeros((8, HB), F32)] * 3
        kept = []
        preact = product(0)
        for r in range(PIECES):
            following = product(r + 1) if r + 1 < PIECES else None
            firsts, seconds = [], []
            for q in range(0, ROWS, STRIP):
                slopes, active, flat = [], [], []
                for base in (0, ROWS):
                    value = preact[base + q:base + q + STRIP]
                    square = value * value
                    inner = value * (GELU_A + GELU_B * square)
                    half = 0.5 * jnp.tanh(inner)
                    gate = 0.5 + half
                    active.append(value * gate)
                    slopes.append(gate + active[-1] * (
                        (0.5 - half) * (2.0 * GELU_A + (6.0 * GELU_B) * square)))
                    flat.append(jnp.where(value > FLAT_FROM, 1.0, 0.0))
                pair = active[0] + active[1]
                mean = (pair * 0.5).astype(BF16)
                for k in range(HB // 128):
                    held[slot, k, r * ROWS + q:r * ROWS + q + STRIP, :] = (
                        mean[:, 128 * k:128 * (k + 1)])
                for k, both in enumerate((pair, flat[0] + flat[1], slopes[0] + slopes[1])):
                    counts[k] = counts[k] + jnp.sum(both.reshape(STRIP // 8, 8, HB), axis=0)
                firsts.append(slopes[0].astype(BF16))
                seconds.append(slopes[1].astype(BF16))
            kept.extend(firsts + seconds)
            if (r + 1) % DEPTH == 0:
                columns = range(2 * (r + 1 - DEPTH), 2 * (r + 1))
                update = mul(
                    jnp.concatenate([patches_t[k] for k in columns], axis=1),
                    jnp.concatenate(kept, axis=0))
                if r + 1 == DEPTH:
                    grad_t[...] = update
                else:
                    grad_t[...] += update
                kept = []
            preact = following
        for k in range(3):
            total[n, k] = counts[k]
        for copy in encoded_copies(n):
            copy.start()

        @pl.when(n == BANDS - 1)
        def _():
            for band in range(BANDS):
                for k in range(3):
                    at = H * k + HB * band
                    own_sum[:, at:at + HB] = jnp.sum(total[band, k], axis=0, keepdims=True)

            def start_sum(i, _):
                sum_copy(i, me).start()
                return 0

            lax.fori_loop(1, NSEQ, start_sum, 0)
            all_sums[me] = own_sum[...]

        grad = grad_t[...].T.reshape(2, CHIPS, 2, 8, K * C)
        for e in range(2):
            grads[n, e, :, 0:8, :] = grad[0, :, e]
            grads[n, e, :, 8:16, :] = grad[1, :, e]
        core_copy(n).start()

        @pl.when(n >= 1)
        def _():
            pass_on(n - 1)

        return 0

    lax.fori_loop(0, BANDS, forward, 0)

    def grp_copy(i, slot):
        peer = lax.rem(grp + i, NGRP)
        return pltpu.make_async_remote_copy(
            src_ref=ready.at[peer], dst_ref=grp_in.at[slot], send_sem=s_grp.at[i],
            recv_sem=r_grp.at[i], device_id={"grp": peer}, device_id_type=MESH)

    def hand_over(n):
        def wait_chip(i, _):
            chip_copy(n, i, lax.rem(chip - i + CHIPS, CHIPS)).wait_recv()
            return 0

        lax.fori_loop(1, CHIPS, wait_chip, 0)
        chip_in[n, chip] = grads[n, core, chip] + core_in[n, chip]
        whole = chip_in[n, 0]
        for j in range(1, CHIPS):
            whole = whole + chip_in[n, j]
        for k in range(2):
            g = 2 * n + k
            ready[g] = whole[8 * k:8 * (k + 1)]
            i = lax.rem(g - grp + NGRP, NGRP)

            @pl.when(i > 0)
            def _():
                grp_copy(i, grp).start()

    def wait_sum(i, _):
        sum_copy(i, lax.rem(me - i + NSEQ, NSEQ)).wait_recv()
        return 0

    pass_on(BANDS - 1)
    hand_over(0)
    lax.fori_loop(1, NSEQ, wait_sum, 0)
    sums = jnp.sum(all_sums[...], axis=0)
    pooled = sums[:, :H] * (1.0 / SEQLEN)
    share = jnp.minimum(sums[:, H:2 * H] / jnp.maximum(sums[:, 2 * H:], 1.0), 1.0)
    left, thirds = pooled, []
    for _ in range(3):
        thirds.append(left.astype(BF16).astype(F32))
        left = left - thirds[-1]
    thirds = jnp.concatenate(thirds + [jnp.zeros((5, H), F32)], axis=0).astype(BF16)
    latent = jnp.sum(mul(thirds, proj[...]), axis=0, keepdims=True)
    for g in range(NGRP):
        at = slice(128 * g, 128 * (g + 1))
        notes[g] = jnp.concatenate([latent, pooled[:, at], share[:, at]], axis=1)

    def own_copy(i, slot):
        peer = lax.rem(grp + i, NGRP)
        return pltpu.make_async_remote_copy(
            src_ref=notes.at[peer], dst_ref=own_notes.at[slot], send_sem=s_own.at[i],
            recv_sem=r_own.at[i], device_id={"grp": peer}, device_id_type=MESH)

    def other_copy(i, slot):
        peer = lax.rem(grp + i, NGRP)
        return pltpu.make_async_remote_copy(
            src_ref=notes.at[peer], dst_ref=other_notes.at[slot], send_sem=s_oth.at[i],
            recv_sem=r_oth.at[i], device_id={"pair": other, "grp": peer}, device_id_type=MESH)

    def start_notes(i, _):
        @pl.when(i > 0)
        def _():
            own_copy(i, grp).start()

        other_copy(i, grp).start()
        return 0

    lax.fori_loop(0, NGRP, start_notes, 0)
    own_notes[grp] = notes[grp]

    for n in range(1, BANDS):
        hand_over(n)
    grp_in[grp] = ready[grp]

    def wait_notes(i, _):
        source = lax.rem(grp - i + NGRP, NGRP)

        @pl.when(i > 0)
        def _():
            own_copy(i, source).wait_recv()

        other_copy(i, source).wait_recv()
        return 0

    lax.fori_loop(0, NGRP, wait_notes, 0)
    for g in range(NGRP):
        own_rows[g:g + 1, :] = own_notes[g]
        other_rows[g:g + 1, :] = other_notes[g]
    z_own, z_other = own_rows[:, :E], other_rows[:, :E]
    scale = lax.rsqrt(jnp.sum(z_own * z_own, axis=1, keepdims=True) + 1e-06)
    scale_other = lax.rsqrt(jnp.sum(z_other * z_other, axis=1, keepdims=True) + 1e-06)
    e_own, e_other = z_own * scale, z_other * scale_other
    time_emb = jnp.where(is_time, e_own, e_other)
    freq_emb = jnp.where(is_time, e_other, e_own)
    dot = functools.partial(lax.dot_general, precision=HIGHEST, preferred_element_type=F32)
    logits = dot(time_emb, freq_emb, (((1,), (1,)), ((), ()))) * (1.0 / TAU)
    row = lax.broadcasted_iota(jnp.int32, (NGRP, NGRP), 0)
    col = lax.broadcasted_iota(jnp.int32, (NGRP, NGRP), 1)
    target = jnp.zeros((NGRP, NGRP), F32)
    for i in range(NGRP):
        target = jnp.where(jnp.logical_and(row == i, col == positives[i]), 1.0, target)
    exponent = jnp.exp(logits)
    by_row = jnp.sum(exponent, axis=1, keepdims=True)
    by_col = jnp.sum(exponent, axis=0, keepdims=True)
    slope = (exponent / by_row + exponent / by_col - 2.0 * target) * (
        LOSS_SCALE / (TAU * 2 * NGRP))
    d_time = dot(slope, freq_emb, (((1,), (0,)), ((), ())))
    d_freq = dot(slope, time_emb, (((0,), (0,)), ((), ())))
    d_emb = jnp.where(is_time, d_time, d_freq)
    along = jnp.sum(z_own * d_emb, axis=1, keepdims=True)
    d_latent = scale * d_emb - z_own * (scale * scale * scale * along)
    own_proj = table[pl.ds(pl.multiple_of(8 * me, 8), 8), :] * (1.0 / SEQLEN)
    take = jnp.where(
        lax.broadcasted_iota(jnp.int32, (8, 128), 1)
        == 8 * me + lax.broadcasted_iota(jnp.int32, (8, 128), 0), 1.0, 0.0)
    shares = dot(take, own_rows[:, 2 * E:], (((1,), (1,)), ((), ())))
    exact = jnp.concatenate([
        jnp.sum(own_proj * d_latent[g:g + 1], axis=1, keepdims=True) for g in range(NGRP)], axis=1)
    blend = exact + shares * (exact.astype(BF16).astype(F32) - exact)
    factors = [blend[:, g:g + 1] for g in range(NGRP)]

    picked = jnp.sum(jnp.sum(target * logits, axis=1, keepdims=True), axis=0, keepdims=True)
    lse = jnp.sum(jnp.log(by_row), axis=0, keepdims=True) + jnp.sum(
        jnp.log(by_col), axis=1, keepdims=True)
    loss_out[...] = (lse - 2.0 * picked) * (1.0 / (2 * NGRP))
    proj_out[0] = dot(own_rows[:, E:2 * E], d_latent, (((0,), (0,)), ((), ())))
    def wait_grp(i, _):
        grp_copy(i, lax.rem(grp - i + NGRP, NGRP)).wait_recv()
        return 0

    lax.fori_loop(1, NGRP, wait_grp, 0)
    result = grp_in[0] * factors[0]
    for g in range(1, NGRP):
        result = result + grp_in[g] * factors[g]
    conv_out[0] = result
    for n in range(BANDS - 2, BANDS):
        for copy in encoded_copies(n):
            copy.wait()

    def sent_seq(i, _):
        for view, main, edge in ((0, time_main, time_halo), (1, freq_main, freq_halo)):
            @pl.when(jnp.logical_or(i > 0, branch != view))
            def _():
                for copy in view_copies(view, i, main, edge, mine):
                    copy.wait_send()

        @pl.when(i > 0)
        def _():
            series_copy(i, me).wait_send()
            sum_copy(i, me).wait_send()
        return 0

    def sent_grp(i, _):
        @pl.when(i > 0)
        def _():
            for n in range(BANDS):
                chip_copy(n, i, chip).wait_send()
            own_copy(i, grp).wait_send()
            grp_copy(i, grp).wait_send()

        other_copy(i, grp).wait_send()
        return 0

    lax.fori_loop(0, NSEQ, sent_seq, 0)
    for n in range(BANDS):
        core_copy(n).wait_send()

    lax.fori_loop(0, CHIPS, sent_grp, 0)


def finish_kernel(*refs):
    sems = refs[8]
    copies = [pltpu.make_async_copy(refs[n], refs[4 + n], sems.at[n]) for n in range(4)]
    for copy in copies:
        copy.start()
    for copy in copies:
        copy.wait()


def body(series, time_blocks, freq_blocks, positives, conv_weight, proj_weight):
    vmem = pl.BlockSpec(memory_space=pltpu.VMEM)
    hbm = pl.BlockSpec(memory_space=pltpu.HBM)
    anywhere = pl.BlockSpec(memory_space=pl.ANY)
    tables = [jnp.asarray(t) for t in transform_tables()]
    sources = NPAIR * NSEQ
    dma = pltpu.SemaphoreType.DMA
    part = (BANDS, CHIPS, 16, K * C)
    main, edge = (NSEQ, 2, 16, 128), (NSEQ, OWN, 256)
    encoded, conv_share, proj_share, loss = pl.pallas_call(
        step_kernel,
        out_shape=(
            jax.ShapeDtypeStruct((1, 1, PAIRS, H), BF16),
            jax.ShapeDtypeStruct((1, 8, K * C), F32),
            jax.ShapeDtypeStruct((1, H // NGRP, E), F32),
            jax.ShapeDtypeStruct((1, 1), F32),
        ),
        in_specs=[hbm] * 11,
        out_specs=(anywhere, vmem, vmem, vmem),
        scratch_shapes=[
            pltpu.SMEM((NGRP,), jnp.int32),
            pltpu.SMEM((1, 16), jnp.int32),
            pltpu.SMEM((1, 16), jnp.int32),
            pltpu.VMEM((OWN * NSEQ, SPAN), F32),
            pltpu.VMEM((K // 2, H, 128), BF16),
            pltpu.VMEM((H, E), BF16),
            *[pltpu.VMEM(t.shape, t.dtype) for t in tables],
            pltpu.VMEM((NSEQ * OWN * 16, 128), F32),
            pltpu.VMEM((NSEQ, OWN * 16, 128), F32),
            pltpu.VMEM((128, 128), F32),
            pltpu.VMEM(main, BF16),
            pltpu.VMEM(edge, F32),
            pltpu.VMEM(main, BF16),
            pltpu.VMEM(edge, F32),
            pltpu.VMEM((sources, 2, 16, 128), BF16),
            pltpu.VMEM((sources, OWN, 256), F32),
            pltpu.VMEM((8 * 2 * C, 128), F32),
            pltpu.VMEM((2 * C, 128), F32),
            pltpu.VMEM((2 * C, 256 + PAIRS), F32),
            pltpu.VMEM((16 + PAIRS, 128), F32),
            pltpu.VMEM((16 + PAIRS, 128), F32),
            pltpu.VMEM((PIECES, K // 2, 2 * ROWS, 128), BF16),
            pltpu.VMEM((2 * PIECES, K * C, 128), BF16),
            pltpu.VMEM((2, HB // 128, PAIRS, 128), BF16),
            pltpu.VMEM((BANDS, 3, 8, HB), F32),
            pltpu.VMEM((K * C, HB), F32),
            pltpu.VMEM((1, 3 * H), F32),
            pltpu.VMEM((NSEQ, 1, 3 * H), F32),
            pltpu.VMEM((NGRP, 1, 3 * E), F32),
            pltpu.VMEM((NGRP, 1, 3 * E), F32),
            pltpu.VMEM((NGRP, 1, 3 * E), F32),
            pltpu.VMEM((NGRP, 3 * E), F32),
            pltpu.VMEM((NGRP, 3 * E), F32),
            pltpu.VMEM((128, E), F32),
            pltpu.VMEM((BANDS, 2, CHIPS, 16, K * C), F32),
            pltpu.VMEM(part, F32),
            pltpu.VMEM(part, F32),
            pltpu.VMEM(part, F32),
            pltpu.VMEM((NGRP, 8, K * C), F32),
            pltpu.VMEM((NGRP, 8, K * C), F32),
            dma((14,)), dma((2, 2)),
            dma((NSEQ,)), dma((NSEQ,)),
            dma((sources,)), dma((sources,)), dma((sources,)), dma((sources,)),
            dma((NSEQ,)), dma((NSEQ,)),
            dma((NGRP,)), dma((NGRP,)),
            dma((NGRP,)), dma((NGRP,)),
            dma((BANDS,)), dma((BANDS,)),
            dma((BANDS, CHIPS)), dma((BANDS, CHIPS)),
            dma((NGRP,)), dma((NGRP,)),
        ],
        compiler_params=pltpu.CompilerParams(
            collective_id=0, has_side_effects=True, vmem_limit_bytes=48 * 1024 * 1024),
        name="step",
    )(*[
        pltpu.with_memory_space_constraint(x, pltpu.HBM)
        for x in (positives, time_blocks, freq_blocks, series[0].T, conv_weight, proj_weight, *tables)
    ])
    outs = [
        pltpu.with_memory_space_constraint(x, pltpu.VMEM)
        for x in (encoded, conv_share, proj_share, loss)
    ]
    encoded, conv_share, proj_share, loss = pl.pallas_call(
        finish_kernel,
        out_shape=[jax.ShapeDtypeStruct(x.shape, x.dtype) for x in outs],
        in_specs=[pl.BlockSpec(memory_space=pltpu.VMEM)] * 4,
        out_specs=[pl.BlockSpec(memory_space=pltpu.HBM)] * 4,
        scratch_shapes=[dma((4,))],
        name="finish",
    )(*outs)
    return (encoded, loss[0, 0], conv_share, proj_share)


def solution(mesh):
    in_specs = (
        P("grp", "seq", "pair"),
        P("grp", None),
        P("grp", None),
        P(),
        P("pair", None, None),
        P("pair", None, None),
    )
    out_specs = (
        P("pair", "grp", "seq", None),
        P(),
        P("pair", ("grp", "seq"), None),
        P("pair", "grp", None),
    )
    return jax.shard_map(body, mesh=mesh, in_specs=in_specs, out_specs=out_specs, check_vma=False)
```

```python
import functools
import math

import jax
import jax.numpy as jnp
import numpy as np
from jax import lax
from jax.experimental import pallas as pl
from jax.experimental.pallas import tpu as pltpu
from jax.sharding import PartitionSpec as P

MESH = pl.DeviceIdType.MESH
F32 = jnp.float32
BF16 = jnp.bfloat16
HIGHEST = lax.Precision.HIGHEST

C = 64
H = 1024
E = 128
K = 8
SEQLEN = 32768
NSEQ = 16
NGRP = 8
NPAIR = 2
OWN = 2
SPAN = SEQLEN // NSEQ
PAIRS = SPAN // 2
BLOCKS = SPAN // 256
TAU = 0.2
LOSS_SCALE = 256.0
GELU_A = math.sqrt(2.0 / math.pi)
GELU_B = 0.044715 * GELU_A
CHIPS = NSEQ // 2
HB = 256
BANDS = H // HB
ROWS = 128
PIECES = PAIRS // ROWS
FLAT_FROM = 3.4
STRIP = 16
DEPTH = 1


def split(values):
    high = values.astype(np.float32).astype(BF16)
    low = (values - high.astype(np.float64)).astype(np.float32).astype(BF16)
    return high, low


def transform_tables():
    row = np.arange(256)
    a = (row // 16) * 16 + 2 * (row % 8) + (row % 16) // 8
    col = np.arange(256)
    k1 = 2 * (col % 128) + col // 128
    first = 2 * np.pi * ((a[:, None] * k1[None, :]) % 256) / 256
    first = np.concatenate([np.cos(first), -np.sin(first)], axis=1)
    b = np.arange(128)
    turn = 2 * np.pi * (b[:, None] * k1[None, :]) / SEQLEN
    turn = np.concatenate([np.cos(turn), np.sin(turn)], axis=1).astype(np.float32)
    k2 = np.arange(128)
    second = 2 * np.pi * ((k2[:, None] * b[None, :]) % 128) / 128
    cos, sin = np.cos(second), np.sin(second)
    second = np.block([[cos, sin], [-sin, cos]])
    pick = np.zeros((2, 128, 256), np.float32)
    for odd_row in range(2):
        for step in range(128):
            pick[odd_row, step, 128 * (step % 2) + 64 * odd_row + step // 2] = 1.0
    return (*split(first), turn, np.concatenate(split(second), axis=0), pick.astype(BF16))


def halves(values):
    high = values.astype(BF16)
    return high, (values - high.astype(F32)).astype(BF16)


def mul(a, b):
    return jnp.dot(a, b, preferred_element_type=F32)


def step_kernel(
    positives_in, time_blocks_in, freq_blocks_in, series_in, weight_in, proj_in,
    first_h_in, first_l_in, turn_in, second_in, pick_in,
    encoded, conv_out, proj_out, loss_out,
    positives, time_blocks, freq_blocks, raw, weight, proj, first_h, first_l, turn, second, pick,
    send, series, rows, time_main, time_halo, freq_main, freq_halo, feat, halo,
    tall, edges, wide, turned, across, patches, patches_t, held, total, grad_t,
    own_sum, all_sums, notes, own_notes, other_notes, own_rows, other_rows, table,
    grads, core_in, passed, chip_in, ready, grp_in,
    s_in, s_enc, s1, r1, s2, r2, s3, r3,
    s_sum, r_sum, s_own, r_own, s_oth, r_oth, s_core, r_core, s_chip, r_chip, s_grp, r_grp,
):
    me = lax.axis_index("seq")
    branch = lax.axis_index("pair")
    grp = lax.axis_index("grp")
    other = 1 - branch
    chip, core = me // 2, lax.rem(me, 2)
    sibling = me + 1 - 2 * core
    is_time = branch == 0

    loads = [
        pltpu.make_async_copy(src, dst, s_in.at[n])
        for n, (src, dst) in enumerate((
            (series_in, raw), (pick_in, pick), (first_h_in, first_h), (first_l_in, first_l),
            (turn_in, turn), (second_in, second),
            *[(weight_in.at[0, :, 128 * j:128 * (j + 1)], weight.at[j]) for j in range(K // 2)],
            (proj_in.at[0], proj), (positives_in, positives), (time_blocks_in, time_blocks),
            (freq_blocks_in, freq_blocks)))
    ]
    loads[0].start()

    barrier = pltpu.get_barrier_semaphore()

    def greet_seq(i, _):
        peer = lax.rem(me + i, NSEQ)

        @pl.when(i > 0)
        def _():
            pl.semaphore_signal(barrier, 1, device_id={"seq": peer}, device_id_type=MESH)

        pl.semaphore_signal(barrier, 1, device_id={"pair": other, "seq": peer}, device_id_type=MESH)
        return 0

    def greet_grp(i, _):
        peer = lax.rem(grp + i, NGRP)
        pl.semaphore_signal(barrier, 1, device_id={"grp": peer}, device_id_type=MESH)
        pl.semaphore_signal(barrier, 1, device_id={"pair": other, "grp": peer}, device_id_type=MESH)
        return 0

    lax.fori_loop(0, NSEQ, greet_seq, 0)
    lax.fori_loop(1, NGRP, greet_grp, 0)
    for load in loads[1:]:
        load.start()

    loads[0].wait()
    for q in range(BLOCKS):
        for odd in range(2):
            at = 128 * (2 * q + odd)
            send[pl.ds(8 * odd + q, NSEQ * OWN, stride=16), :] = raw[:, at:at + 128]
    pl.semaphore_wait(barrier, 2 * NSEQ - 1 + 2 * (NGRP - 1))

    def series_copy(i, dst):
        peer = lax.rem(me + i, NSEQ)
        return pltpu.make_async_remote_copy(
            src_ref=send.at[pl.ds(pl.multiple_of(32 * peer, 32), 32)], dst_ref=series.at[dst],
            send_sem=s1.at[i], recv_sem=r1.at[i], device_id={"seq": peer}, device_id_type=MESH)

    def start_series(i, _):
        series_copy(i, me).start()
        return 0

    lax.fori_loop(1, NSEQ, start_series, 0)
    series[me] = send[pl.ds(pl.multiple_of(32 * me, 32), 32), :]
    for load in loads[1:]:
        load.wait()
    table[...] = proj[pl.ds(pl.multiple_of(128 * grp, 128), 128), :].astype(F32)

    def wait_series(i, _):
        series_copy(i, lax.rem(me - i + NSEQ, NSEQ)).wait_recv()
        return 0

    lax.fori_loop(1, NSEQ, wait_series, 0)

    lane = lax.broadcasted_iota(jnp.int32, (NSEQ, 128), 1)

    def pack(values, main, edge):
        parts = [v.reshape(NSEQ, BLOCKS, 256) for v in values]
        block = jnp.concatenate(parts, axis=1).astype(BF16)
        main[:, 0] = block[:, :, :128]
        main[:, 1] = block[:, :, 128:]
        for c in range(OWN):
            for half in range(2):
                columns = slice(128 * half, 128 * (half + 1))
                rows[...] = values[c][:, columns]
                low = rows[pl.ds(0, NSEQ, stride=BLOCKS), :]
                high = rows[pl.ds(BLOCKS - 1, NSEQ, stride=BLOCKS), :]
                before = pltpu.roll(high, 1, 0)
                after = pltpu.roll(low, NSEQ - 1, 0)
                both = jnp.where(lane >= 64, before, after)
                for d in range(NSEQ):
                    edge[d, c:c + 1, columns] = both[d:d + 1]

    def view_copies(view, i, main, edge, slot):
        peer = lax.rem(me + i, NSEQ)
        target = {"pair": view, "seq": peer}
        n = view * NSEQ + i
        return (
            pltpu.make_async_remote_copy(
                src_ref=main.at[peer], dst_ref=feat.at[slot], send_sem=s2.at[n],
                recv_sem=r2.at[branch * NSEQ + i], device_id=target, device_id_type=MESH),
            pltpu.make_async_remote_copy(
                src_ref=edge.at[peer], dst_ref=halo.at[slot], send_sem=s3.at[n],
                recv_sem=r3.at[branch * NSEQ + i], device_id=target, device_id_type=MESH),
        )

    mine = branch * NSEQ + me

    def start_view(view, main, edge):
        def step(i, _):
            @pl.when(jnp.logical_or(i > 0, branch != view))
            def _():
                for copy in view_copies(view, i, main, edge, mine):
                    copy.start()
            return 0

        lax.fori_loop(0, NSEQ, step, 0)

        @pl.when(branch == view)
        def _():
            feat[mine] = main[me]
            halo[mine] = edge[me]

    flats = []
    for c in range(OWN):
        whole = series[:, 16 * c:16 * c + 16, :].reshape(256, 128)
        flats.append(jnp.concatenate([whole[:128].T, whole[128:].T], axis=1))
    high, low = halves(jnp.concatenate(flats, axis=0))
    part = mul(high, first_h[...]) + (mul(high, first_l[...]) + mul(low, first_h[...]))
    re, im = part[:, :256], part[:, 256:]
    cos = jnp.concatenate([turn[:, :256]] * OWN, axis=0)
    sin = jnp.concatenate([turn[:, 256:]] * OWN, axis=0)
    spun_re, spun_im = re * cos + im * sin, im * cos - re * sin
    powers = []
    for c in range(OWN):
        at = slice(128 * c, 128 * (c + 1))
        high, low = halves(jnp.concatenate([spun_re[at], spun_im[at]], axis=0))
        both = mul(second[...], high)
        spec = both[:256] + (both[256:] + mul(second[:256, :], low))
        re, im = spec[:128], spec[128:]
        powers.append(jnp.sqrt(1.0 + (re * re + im * im) * (1.0 / SEQLEN)))
    pack(powers, freq_main, freq_halo)
    start_view(1, freq_main, freq_halo)

    even = [series[:, 16 * c:16 * c + 8, :].reshape(128, 128) for c in range(OWN)]
    odd = [series[:, 16 * c + 8:16 * c + 16, :].reshape(128, 128) for c in range(OWN)]
    views = [
        jnp.dot(even[c].astype(BF16), pick[0], preferred_element_type=F32)
        + jnp.dot(odd[c].astype(BF16), pick[1], preferred_element_type=F32)
        for c in range(OWN)
    ]
    pack(views, time_main, time_halo)
    start_view(0, time_main, time_halo)

    def wait_view(i, _):
        peer = lax.rem(me - i + NSEQ, NSEQ)

        def arrivals(source):
            slot = source * NSEQ + peer
            target = {"pair": source, "seq": peer}
            return (
                pltpu.make_async_remote_copy(
                    src_ref=freq_main.at[peer], dst_ref=feat.at[slot], send_sem=s2.at[i],
                    recv_sem=r2.at[source * NSEQ + i], device_id=target, device_id_type=MESH),
                pltpu.make_async_remote_copy(
                    src_ref=freq_halo.at[peer], dst_ref=halo.at[slot], send_sem=s3.at[i],
                    recv_sem=r3.at[source * NSEQ + i], device_id=target, device_id_type=MESH),
            )

        @pl.when(i > 0)
        def _():
            for copy in arrivals(branch):
                copy.wait_recv()

        for copy in arrivals(other):
            copy.wait_recv()
        return 0

    lax.fori_loop(0, NSEQ, wait_view, 0)

    listed = [jnp.where(is_time, time_blocks[0, n], freq_blocks[0, n]) for n in range(16)]

    def keep(q):
        block = me * BLOCKS + q
        hit = listed[0] == block
        for n in range(1, 16):
            hit = jnp.logical_or(hit, listed[n] == block)
        drop = jnp.logical_or(hit, jnp.logical_or(block < 0, block >= NSEQ * BLOCKS))
        return jnp.where(drop, 0.0, 1.0).astype(F32)

    for parity in range(2):
        tall[parity * 512:(parity + 1) * 512, :] = feat[:, parity].astype(F32).reshape(512, 128)
        for source in range(NPAIR * NSEQ):
            edges[parity * C + OWN * source:parity * C + OWN * (source + 1), :] = (
                halo[source, :, parity * 128:(parity + 1) * 128])
    side = lax.broadcasted_iota(jnp.int32, (128, 128), 1)
    rim = edges[...].astype(BF16).astype(F32) * jnp.where(side >= 64, keep(-1), keep(BLOCKS))
    wide[:, 0:128] = rim
    wide[:, 128 + PAIRS:256 + PAIRS] = rim
    rim_t = rim.T
    turned[0:8, :] = rim_t[120:128]
    turned[8 + PAIRS:16 + PAIRS, :] = rim_t[0:8]
    for q in range(BLOCKS):
        piece = tall[pl.ds(q, 128, stride=BLOCKS), :] * keep(q)
        wide[:, 128 * (q + 1):128 * (q + 2)] = piece
        turned[8 + 128 * q:8 + 128 * (q + 1), :] = piece.T
    across[...] = pltpu.roll(turned[...], 64, 1)
    low_half = lax.broadcasted_iota(jnp.int32, (ROWS, 128), 1) < 64
    for j in range(K // 2):
        for r in range(PIECES):
            at = 8 + j - 2 + ROWS * r
            patches[r, j, 0:ROWS, :] = turned[at:at + ROWS, :].astype(BF16)
            patches[r, j, ROWS:2 * ROWS, :] = jnp.where(
                low_half, across[at:at + ROWS, :], across[at + 1:at + 1 + ROWS, :]).astype(BF16)
    for d in range(-2, 3):
        whole = wide[...]
        if d != 0:
            whole = pltpu.roll(whole, (-d) % (256 + PAIRS), 1)
        part = whole[:, 128:128 + PAIRS].astype(BF16)
        j = d + 2
        for r in range(PIECES):
            chunk = part[:, ROWS * r:ROWS * (r + 1)]
            if j < K // 2:
                patches_t[2 * r, 128 * j:128 * (j + 1), :] = chunk
                patches_t[2 * r + 1, 128 * j:128 * j + 64, :] = chunk[64:]
            if j > 0:
                patches_t[2 * r + 1, 128 * (j - 1) + 64:128 * j, :] = chunk[:64]

    def encoded_copies(n):
        slot = lax.rem(n, 2)
        return [
            pltpu.make_async_copy(
                held.at[slot, k],
                encoded.at[0, 0, :, pl.ds(pl.multiple_of(n * HB + 128 * k, 128), 128)],
                s_enc.at[slot, k])
            for k in range(HB // 128)
        ]

    def core_copy(n):
        return pltpu.make_async_remote_copy(
            src_ref=grads.at[n, 1 - core], dst_ref=core_in.at[n], send_sem=s_core.at[n],
            recv_sem=r_core.at[n], device_id={"seq": sibling}, device_id_type=MESH)

    def chip_copy(n, i, slot):
        j = lax.rem(chip + i, CHIPS)
        return pltpu.make_async_remote_copy(
            src_ref=passed.at[n, j], dst_ref=chip_in.at[n, slot], send_sem=s_chip.at[n, i],
            recv_sem=r_chip.at[n, i], device_id={"seq": 2 * j + core}, device_id_type=MESH)

    def sum_copy(i, slot):
        return pltpu.make_async_remote_copy(
            src_ref=own_sum, dst_ref=all_sums.at[slot], send_sem=s_sum.at[i],
            recv_sem=r_sum.at[i], device_id={"seq": lax.rem(me + i, NSEQ)}, device_id_type=MESH)

    def pass_on(n):
        core_copy(n).wait_recv()

        def one(i, _):
            j = lax.rem(chip + i, CHIPS)
            passed[n, j] = grads[n, core, j] + core_in[n, j]
            chip_copy(n, i, chip).start()
            return 0

        lax.fori_loop(1, CHIPS, one, 0)

    def forward(n, _):
        at = pl.ds(pl.multiple_of(n * HB, HB), HB)
        weights = jnp.concatenate([weight[j, at, :] for j in range(K // 2)], axis=1)

        @pl.when(n >= 2)
        def _():
            for copy in encoded_copies(n):
                copy.wait()

        slot = lax.rem(n, 2)

        def product(r):
            rows = jnp.concatenate([patches[r, j] for j in range(K // 2)], axis=1)
            return lax.dot_general(
                rows, weights, (((1,), (1,)), ((), ())), preferred_element_type=F32)

        counts = [jnp.zeros((8, HB), F32)] * 3
        kept = []
        preact = product(0)
        for r in range(PIECES):
            following = product(r + 1) if r + 1 < PIECES else None
            firsts, seconds = [], []
            for q in range(0, ROWS, STRIP):
                slopes, active, flat = [], [], []
                for base in (0, ROWS):
                    value = preact[base + q:base + q + STRIP]
                    square = value * value
                    inner = value * (GELU_A + GELU_B * square)
                    half = 0.5 * jnp.tanh(inner)
                    gate = 0.5 + half
                    active.append(value * gate)
                    slopes.append(gate + active[-1] * (
                        (0.5 - half) * (2.0 * GELU_A + (6.0 * GELU_B) * square)))
                    flat.append(jnp.where(value > FLAT_FROM, 1.0, 0.0))
                pair = active[0] + active[1]
                mean = (pair * 0.5).astype(BF16)
                for k in range(HB // 128):
                    held[slot, k, r * ROWS + q:r * ROWS + q + STRIP, :] = (
                        mean[:, 128 * k:128 * (k + 1)])
                for k, both in enumerate((pair, flat[0] + flat[1], slopes[0] + slopes[1])):
                    counts[k] = counts[k] + jnp.sum(both.reshape(STRIP // 8, 8, HB), axis=0)
                firsts.append(slopes[0].astype(BF16))
                seconds.append(slopes[1].astype(BF16))
            kept.extend(firsts + seconds)
            if (r + 1) % DEPTH == 0:
                columns = range(2 * (r + 1 - DEPTH), 2 * (r + 1))
                update = mul(
                    jnp.concatenate([patches_t[k] for k in columns], axis=1),
                    jnp.concatenate(kept, axis=0))
                if r + 1 == DEPTH:
                    grad_t[...] = update
                else:
                    grad_t[...] += update
                kept = []
            preact = following
        for k in range(3):
            total[n, k] = counts[k]
        for copy in encoded_copies(n):
            copy.start()

        @pl.when(n == BANDS - 1)
        def _():
            for band in range(BANDS):
                for k in range(3):
                    at = H * k + HB * band
                    own_sum[:, at:at + HB] = jnp.sum(total[band, k], axis=0, keepdims=True)

            def start_sum(i, _):
                sum_copy(i, me).start()
                return 0

            lax.fori_loop(1, NSEQ, start_sum, 0)
            all_sums[me] = own_sum[...]

        grad = grad_t[...].T.reshape(2, CHIPS, 2, 8, K * C)
        for e in range(2):
            grads[n, e, :, 0:8, :] = grad[0, :, e]
            grads[n, e, :, 8:16, :] = grad[1, :, e]
        core_copy(n).start()

        @pl.when(n >= 1)
        def _():
            pass_on(n - 1)

        return 0

    lax.fori_loop(0, BANDS, forward, 0)

    def grp_copy(i, slot):
        peer = lax.rem(grp + i, NGRP)
        return pltpu.make_async_remote_copy(
            src_ref=ready.at[peer], dst_ref=grp_in.at[slot], send_sem=s_grp.at[i],
            recv_sem=r_grp.at[i], device_id={"grp": peer}, device_id_type=MESH)

    def hand_over(n):
        def wait_chip(i, _):
            chip_copy(n, i, lax.rem(chip - i + CHIPS, CHIPS)).wait_recv()
            return 0

        lax.fori_loop(1, CHIPS, wait_chip, 0)
        chip_in[n, chip] = grads[n, core, chip] + core_in[n, chip]
        whole = chip_in[n, 0]
        for j in range(1, CHIPS):
            whole = whole + chip_in[n, j]
        for k in range(2):
            g = 2 * n + k
            ready[g] = whole[8 * k:8 * (k + 1)]
            i = lax.rem(g - grp + NGRP, NGRP)

            @pl.when(i > 0)
            def _():
                grp_copy(i, grp).start()

    def wait_sum(i, _):
        sum_copy(i, lax.rem(me - i + NSEQ, NSEQ)).wait_recv()
        return 0

    pass_on(BANDS - 1)
    hand_over(0)
    lax.fori_loop(1, NSEQ, wait_sum, 0)
    sums = jnp.sum(all_sums[...], axis=0)
    pooled = sums[:, :H] * (1.0 / SEQLEN)
    share = jnp.minimum(sums[:, H:2 * H] / jnp.maximum(sums[:, 2 * H:], 1.0), 1.0)
    left, thirds = pooled, []
    for _ in range(3):
        thirds.append(left.astype(BF16).astype(F32))
        left = left - thirds[-1]
    thirds = jnp.concatenate(thirds + [jnp.zeros((5, H), F32)], axis=0).astype(BF16)
    latent = jnp.sum(mul(thirds, proj[...]), axis=0, keepdims=True)
    for g in range(NGRP):
        at = slice(128 * g, 128 * (g + 1))
        notes[g] = jnp.concatenate([latent, pooled[:, at], share[:, at]], axis=1)

    def own_copy(i, slot):
        peer = lax.rem(grp + i, NGRP)
        return pltpu.make_async_remote_copy(
            src_ref=notes.at[peer], dst_ref=own_notes.at[slot], send_sem=s_own.at[i],
            recv_sem=r_own.at[i], device_id={"grp": peer}, device_id_type=MESH)

    def other_copy(i, slot):
        peer = lax.rem(grp + i, NGRP)
        return pltpu.make_async_remote_copy(
            src_ref=notes.at[peer], dst_ref=other_notes.at[slot], send_sem=s_oth.at[i],
            recv_sem=r_oth.at[i], device_id={"pair": other, "grp": peer}, device_id_type=MESH)

    def start_notes(i, _):
        @pl.when(i > 0)
        def _():
            own_copy(i, grp).start()

        other_copy(i, grp).start()
        return 0

    lax.fori_loop(0, NGRP, start_notes, 0)
    own_notes[grp] = notes[grp]

    for n in range(1, BANDS):
        hand_over(n)
    grp_in[grp] = ready[grp]

    def wait_notes(i, _):
        source = lax.rem(grp - i + NGRP, NGRP)

        @pl.when(i > 0)
        def _():
            own_copy(i, source).wait_recv()

        other_copy(i, source).wait_recv()
        return 0

    lax.fori_loop(0, NGRP, wait_notes, 0)
    for g in range(NGRP):
        own_rows[g:g + 1, :] = own_notes[g]
        other_rows[g:g + 1, :] = other_notes[g]
    z_own, z_other = own_rows[:, :E], other_rows[:, :E]
    scale = lax.rsqrt(jnp.sum(z_own * z_own, axis=1, keepdims=True) + 1e-06)
    scale_other = lax.rsqrt(jnp.sum(z_other * z_other, axis=1, keepdims=True) + 1e-06)
    e_own, e_other = z_own * scale, z_other * scale_other
    time_emb = jnp.where(is_time, e_own, e_other)
    freq_emb = jnp.where(is_time, e_other, e_own)
    dot = functools.partial(lax.dot_general, precision=HIGHEST, preferred_element_type=F32)
    logits = dot(time_emb, freq_emb, (((1,), (1,)), ((), ()))) * (1.0 / TAU)
    row = lax.broadcasted_iota(jnp.int32, (NGRP, NGRP), 0)
    col = lax.broadcasted_iota(jnp.int32, (NGRP, NGRP), 1)
    target = jnp.zeros((NGRP, NGRP), F32)
    for i in range(NGRP):
        target = jnp.where(jnp.logical_and(row == i, col == positives[i]), 1.0, target)
    exponent = jnp.exp(logits)
    by_row = jnp.sum(exponent, axis=1, keepdims=True)
    by_col = jnp.sum(exponent, axis=0, keepdims=True)
    slope = (exponent / by_row + exponent / by_col - 2.0 * target) * (
        LOSS_SCALE / (TAU * 2 * NGRP))
    d_time = dot(slope, freq_emb, (((1,), (0,)), ((), ())))
    d_freq = dot(slope, time_emb, (((0,), (0,)), ((), ())))
    d_emb = jnp.where(is_time, d_time, d_freq)
    along = jnp.sum(z_own * d_emb, axis=1, keepdims=True)
    d_latent = scale * d_emb - z_own * (scale * scale * scale * along)
    own_proj = table[pl.ds(pl.multiple_of(8 * me, 8), 8), :] * (1.0 / SEQLEN)
    take = jnp.where(
        lax.broadcasted_iota(jnp.int32, (8, 128), 1)
        == 8 * me + lax.broadcasted_iota(jnp.int32, (8, 128), 0), 1.0, 0.0)
    shares = dot(take, own_rows[:, 2 * E:], (((1,), (1,)), ((), ())))
    exact = jnp.concatenate([
        jnp.sum(own_proj * d_latent[g:g + 1], axis=1, keepdims=True) for g in range(NGRP)], axis=1)
    blend = exact + shares * (exact.astype(BF16).astype(F32) - exact)
    factors = [blend[:, g:g + 1] for g in range(NGRP)]

    picked = jnp.sum(jnp.sum(target * logits, axis=1, keepdims=True), axis=0, keepdims=True)
    lse = jnp.sum(jnp.log(by_row), axis=0, keepdims=True) + jnp.sum(
        jnp.log(by_col), axis=1, keepdims=True)
    loss_out[...] = (lse - 2.0 * picked) * (1.0 / (2 * NGRP))
    proj_out[0] = dot(own_rows[:, E:2 * E], d_latent, (((0,), (0,)), ((), ())))
    def wait_grp(i, _):
        grp_copy(i, lax.rem(grp - i + NGRP, NGRP)).wait_recv()
        return 0

    lax.fori_loop(1, NGRP, wait_grp, 0)
    result = grp_in[0] * factors[0]
    for g in range(1, NGRP):
        result = result + grp_in[g] * factors[g]
    conv_out[0] = result
    for n in range(BANDS - 2, BANDS):
        for copy in encoded_copies(n):
            copy.wait()

    def sent_seq(i, _):
        for view, main, edge in ((0, time_main, time_halo), (1, freq_main, freq_halo)):
            @pl.when(jnp.logical_or(i > 0, branch != view))
            def _():
                for copy in view_copies(view, i, main, edge, mine):
                    copy.wait_send()

        @pl.when(i > 0)
        def _():
            series_copy(i, me).wait_send()
            sum_copy(i, me).wait_send()
        return 0

    def sent_grp(i, _):
        @pl.when(i > 0)
        def _():
            for n in range(BANDS):
                chip_copy(n, i, chip).wait_send()
            own_copy(i, grp).wait_send()
            grp_copy(i, grp).wait_send()

        other_copy(i, grp).wait_send()
        return 0

    lax.fori_loop(0, NSEQ, sent_seq, 0)
    for n in range(BANDS):
        core_copy(n).wait_send()

    lax.fori_loop(0, CHIPS, sent_grp, 0)


def finish_kernel(*refs):
    sems = refs[8]
    copies = [pltpu.make_async_copy(refs[n], refs[4 + n], sems.at[n]) for n in range(4)]
    for copy in copies:
        copy.start()
    for copy in copies:
        copy.wait()


def body(series, time_blocks, freq_blocks, positives, conv_weight, proj_weight):
    vmem = pl.BlockSpec(memory_space=pltpu.VMEM)
    hbm = pl.BlockSpec(memory_space=pltpu.HBM)
    anywhere = pl.BlockSpec(memory_space=pl.ANY)
    tables = [jnp.asarray(t) for t in transform_tables()]
    sources = NPAIR * NSEQ
    dma = pltpu.SemaphoreType.DMA
    part = (BANDS, CHIPS, 16, K * C)
    main, edge = (NSEQ, 2, 16, 128), (NSEQ, OWN, 256)
    encoded, conv_share, proj_share, loss = pl.pallas_call(
        step_kernel,
        out_shape=(
            jax.ShapeDtypeStruct((1, 1, PAIRS, H), BF16),
            jax.ShapeDtypeStruct((1, 8, K * C), F32),
            jax.ShapeDtypeStruct((1, H // NGRP, E), F32),
            jax.ShapeDtypeStruct((1, 1), F32),
        ),
        in_specs=[hbm] * 11,
        out_specs=(anywhere, vmem, vmem, vmem),
        scratch_shapes=[
            pltpu.SMEM((NGRP,), jnp.int32),
            pltpu.SMEM((1, 16), jnp.int32),
            pltpu.SMEM((1, 16), jnp.int32),
            pltpu.VMEM((OWN * NSEQ, SPAN), F32),
            pltpu.VMEM((K // 2, H, 128), BF16),
            pltpu.VMEM((H, E), BF16),
            *[pltpu.VMEM(t.shape, t.dtype) for t in tables],
            pltpu.VMEM((NSEQ * OWN * 16, 128), F32),
            pltpu.VMEM((NSEQ, OWN * 16, 128), F32),
            pltpu.VMEM((128, 128), F32),
            pltpu.VMEM(main, BF16),
            pltpu.VMEM(edge, F32),
            pltpu.VMEM(main, BF16),
            pltpu.VMEM(edge, F32),
            pltpu.VMEM((sources, 2, 16, 128), BF16),
            pltpu.VMEM((sources, OWN, 256), F32),
            pltpu.VMEM((8 * 2 * C, 128), F32),
            pltpu.VMEM((2 * C, 128), F32),
            pltpu.VMEM((2 * C, 256 + PAIRS), F32),
            pltpu.VMEM((16 + PAIRS, 128), F32),
            pltpu.VMEM((16 + PAIRS, 128), F32),
            pltpu.VMEM((PIECES, K // 2, 2 * ROWS, 128), BF16),
            pltpu.VMEM((2 * PIECES, K * C, 128), BF16),
            pltpu.VMEM((2, HB // 128, PAIRS, 128), BF16),
            pltpu.VMEM((BANDS, 3, 8, HB), F32),
            pltpu.VMEM((K * C, HB), F32),
            pltpu.VMEM((1, 3 * H), F32),
            pltpu.VMEM((NSEQ, 1, 3 * H), F32),
            pltpu.VMEM((NGRP, 1, 3 * E), F32),
            pltpu.VMEM((NGRP, 1, 3 * E), F32),
            pltpu.VMEM((NGRP, 1, 3 * E), F32),
            pltpu.VMEM((NGRP, 3 * E), F32),
            pltpu.VMEM((NGRP, 3 * E), F32),
            pltpu.VMEM((128, E), F32),
            pltpu.VMEM((BANDS, 2, CHIPS, 16, K * C), F32),
            pltpu.VMEM(part, F32),
            pltpu.VMEM(part, F32),
            pltpu.VMEM(part, F32),
            pltpu.VMEM((NGRP, 8, K * C), F32),
            pltpu.VMEM((NGRP, 8, K * C), F32),
            dma((14,)), dma((2, 2)),
            dma((NSEQ,)), dma((NSEQ,)),
            dma((sources,)), dma((sources,)), dma((sources,)), dma((sources,)),
            dma((NSEQ,)), dma((NSEQ,)),
            dma((NGRP,)), dma((NGRP,)),
            dma((NGRP,)), dma((NGRP,)),
            dma((BANDS,)), dma((BANDS,)),
            dma((BANDS, CHIPS)), dma((BANDS, CHIPS)),
            dma((NGRP,)), dma((NGRP,)),
        ],
        compiler_params=pltpu.CompilerParams(
            collective_id=0, has_side_effects=True, vmem_limit_bytes=48 * 1024 * 1024),
        name="step",
    )(*[
        pltpu.with_memory_space_constraint(x, pltpu.HBM)
        for x in (positives, time_blocks, freq_blocks, series[0].T, conv_weight, proj_weight, *tables)
    ])
    outs = [
        pltpu.with_memory_space_constraint(x, pltpu.VMEM)
        for x in (encoded, conv_share, proj_share, loss)
    ]
    encoded, conv_share, proj_share, loss = pl.pallas_call(
        finish_kernel,
        out_shape=[jax.ShapeDtypeStruct(x.shape, x.dtype) for x in outs],
        in_specs=[pl.BlockSpec(memory_space=pltpu.VMEM)] * 4,
        out_specs=[pl.BlockSpec(memory_space=pltpu.HBM)] * 4,
        scratch_shapes=[dma((4,))],
        name="finish",
    )(*outs)
    return (encoded, loss[0, 0], conv_share, proj_share)


def solution(mesh):
    in_specs = (
        P("grp", "seq", "pair"),
        P("grp", None),
        P("grp", None),
        P(),
        P("pair", None, None),
        P("pair", None, None),
    )
    out_specs = (
        P("pair", "grp", "seq", None),
        P(),
        P("pair", ("grp", "seq"), None),
        P("pair", "grp", None),
    )
    return jax.shard_map(body, mesh=mesh, in_specs=in_specs, out_specs=out_specs, check_vma=False)
```
